512 devices in a mesh: ctx: 8 (over y), head: 4 (over x), resp: 16 (over z, core).
Axes of the slice: x: 4, y: 8, z: 8, core: 2. Of those that a mesh axis runs over, the one named last changes fastest.
Arguments:
- prompt_query: bfloat16 [8192, 64, 128], P(('ctx', 'head'), 'resp'), may hold values from -6 to 6
- prompt_key: bfloat16 [8192, 64, 128], P(('ctx', 'head'), 'resp'), may hold values from -6 to 6
- prompt_value: bfloat16 [8192, 64, 128], P(('ctx', 'head'), 'resp'), may hold values from -6 to 6
- prompt_cotangent: bfloat16 [8192, 64, 128], P(('ctx', 'head'), 'resp'), may hold values from -6 to 6
- reply_query: bfloat16 [16, 512, 64, 128], P('resp', None, ('ctx', 'head')), may hold values from -6 to 6
- reply_key: bfloat16 [16, 512, 64, 128], P('resp', None, ('ctx', 'head')), may hold values from -6 to 6
- reply_value: bfloat16 [16, 512, 64, 128], P('resp', None, ('ctx', 'head')), may hold values from -6 to 6
- reply_cotangent: bfloat16 [16, 512, 64, 128], P('resp', None, ('ctx', 'head')), may hold values from -6 to 6
- reply_weight: float32 [16], P('resp'), may hold values from 0.5 to 2
- reply_length: int32 [16], P('resp'), may hold values from 1 to 512, 6144 in all
Outputs:
- prompt_output: bfloat16 [8192, 64, 128], P(('ctx', 'head'), 'resp')
- reply_output: bfloat16 [16, 512, 64, 128], P('resp', None, ('ctx', 'head'))
- prompt_query_grad: bfloat16 [8192, 64, 128], P(('ctx', 'head'), 'resp')
- prompt_key_grad: bfloat16 [8192, 64, 128], P(('ctx', 'head'), 'resp')
- prompt_value_grad: bfloat16 [8192, 64, 128], P(('ctx', 'head'), 'resp')
- reply_query_grad: bfloat16 [16, 512, 64, 128], P('resp', None, ('ctx', 'head'))
- reply_key_grad: bfloat16 [16, 512, 64, 128], P('resp', None, ('ctx', 'head'))
- reply_value_grad: bfloat16 [16, 512, 64, 128], P('resp', None, ('ctx', 'head'))
The draws below stay inside these ranges and needn't reach their ends.
Inputs may be any that keep to these rules, and one draw needn't show every extreme that they name: `reply_length`: the longest response has exactly 512 live tokens; the slots of a response from its length on are padding.
All inputs are finite; a program needn't handle non-finite values. No bound on the sum of `reply_length` on one device may be relied on, other than what follows from the above.
Results may differ from the reference program's by a relative error of at most 0.0095.
Values sent between devices are 32-bit elements; how exact they have to be, the bound alone decides.
A program may use at most 128 MiB of HBM per device.

```python
import math
import jax
import jax.numpy as jnp
import numpy as np
from jax import lax

H = 64
E = 128
PROMPT_DEV = 256
L = 512
R = 16
P_SIZE = 8192


def level_of(stream_key, shape, split, low, high):
    factor_of, own = 1.0, jax.random.fold_in(stream_key, 6)
    for axis_at, parts in split:
        draws = jnp.exp(jax.random.uniform(jax.random.fold_in(own, axis_at), (parts,), jnp.float32, low / len(split), high / len(split)))
        factor_of = factor_of * jnp.repeat(draws, shape[axis_at] // parts).reshape([-1 if axis == axis_at else 1 for axis in range(len(shape))])
    return factor_of


def length_profile(count, total, reach, lean):
    portions = [(1 << 20) // math.isqrt(rank ** lean) + 1 for rank in range(2, count + 1)]
    spare, holding = total - reach - (count - 1), [1] * (count - 1)
    while spare > 0:
        candidates = [i for i in range(count - 1) if holding[i] < reach]
        whole, budget = sum([portions[i] for i in candidates]), spare
        for i in candidates:
            more = min(reach - holding[i], max(1, budget * portions[i] // whole), spare)
            holding[i] = holding[i] + more
            spare = spare - more
    return np.array([reach] + holding)


def ragged_sizes(stream_key, number_of, total, limit, lean):
    if number_of == 2:
        one = jax.random.randint(stream_key, (), max(1, total - limit), min(limit, total - 1) + 1)
        return jnp.stack([one, total - one])
    lengths = jnp.asarray(length_profile(number_of, total, limit, lean), jnp.int32)
    couples = (number_of - 1) // 2
    source_of, taker = lengths[1:1 + 2 * couples:2], lengths[2:2 + 2 * couples:2]
    room = jnp.minimum(source_of - 1, limit - taker)
    shifted = jax.random.randint(jax.random.fold_in(stream_key, 1), (couples,), 0, 1 << 20) % (room + 1)
    lengths = lengths.at[1:1 + 2 * couples:2].set(source_of - shifted).at[2:2 + 2 * couples:2].set(taker + shifted)
    return lengths[jax.random.permutation(jax.random.fold_in(stream_key, 2), number_of)]


def centred(own_key, extent, width, most, cuts=(), kind=jnp.bfloat16):
    factor_of = level_of(own_key, extent, cuts, -0.22, 0.18) if cuts else 1.0
    result = jax.random.normal(own_key, extent, jnp.float32) * width * factor_of
    return jnp.minimum(jnp.maximum(result, -most), most).astype(kind)


def setup_inputs(seed: int = 0) -> dict:
    seeds = jax.random.split(jax.random.key(seed), 11)
    return {
        "prompt_query": centred(seeds[0], (P_SIZE, H, E), 1.0, 6.0, ((0, 32), (1, 16))),
        "prompt_key": centred(seeds[1], (P_SIZE, H, E), 1.0, 6.0, ((0, 32), (1, 16))),
        "prompt_value": centred(seeds[2], (P_SIZE, H, E), 1.0, 6.0, ((0, 32), (1, 16))),
        "prompt_cotangent": centred(seeds[3], (P_SIZE, H, E), 1.0, 6.0, ((0, 32), (1, 16))),
        "reply_query": centred(seeds[4], (R, L, H, E), 1.0, 6.0, ((0, 16), (2, 32))),
        "reply_key": centred(seeds[5], (R, L, H, E), 1.0, 6.0, ((0, 16), (2, 32))),
        "reply_value": centred(seeds[6], (R, L, H, E), 1.0, 6.0, ((0, 16), (2, 32))),
        "reply_cotangent": centred(seeds[7], (R, L, H, E), 1.0, 6.0, ((0, 16), (2, 32))),
        "reply_weight": jnp.clip(0.5 + 1.5 * jax.random.uniform(seeds[8], (R,), jnp.float32) ** level_of(seeds[8], (R,), ((0, 16),), -0.2, 0.2), 0.5, 2.0),
        "reply_length": ragged_sizes(seeds[9], R, R * L * 3 // 4, L, 1).astype(jnp.int32),
    }


def position_scale(first_row, row_total):
    positions = (first_row + jnp.arange(row_total, dtype=jnp.int32)).astype(jnp.float32)
    return lax.rsqrt(E * (positions + 1.0))

def causal_mask(row_total):
    return jnp.arange(row_total)[:, None] >= jnp.arange(row_total)[None, :]

def forward_pieces(query, key_rows, value_rows, row_scale):
    causal = causal_mask(query.shape[0])
    scores = jnp.einsum('thd,shd->hts', query.astype(jnp.float32), key_rows.astype(jnp.float32), precision=lax.Precision.HIGHEST)
    mixing = jnp.where(causal[None], scores * row_scale[None, :, None], 0.0).astype(jnp.bfloat16)
    inner_sum = jnp.einsum('hts,she->the', mixing.astype(jnp.float32), value_rows.astype(jnp.float32), precision=lax.Precision.HIGHEST)
    return (mixing, inner_sum)

def carried_term(query, state_in, row_scale):
    product = jnp.einsum('thd,hde->the', query.astype(jnp.float32), state_in, precision=lax.Precision.HIGHEST)
    return row_scale[:, None, None] * product

def local_state(key_rows, value_rows):
    return jnp.einsum('shd,she->hde', key_rows.astype(jnp.float32), value_rows.astype(jnp.float32), precision=lax.Precision.HIGHEST)

def local_moment(query, cotangent, row_scale):
    scaled = query.astype(jnp.float32) * row_scale[:, None, None]
    return jnp.einsum('thd,the->hde', scaled, cotangent.astype(jnp.float32), precision=lax.Precision.HIGHEST)

def backward_pieces(query, key_rows, value_rows, cotangent, mixing, row_scale, state_in, suffix_in):
    causal = causal_mask(query.shape[0])
    cot_wide = cotangent.astype(jnp.float32)
    grad_mixing = jnp.einsum('the,she->hts', cot_wide, value_rows.astype(jnp.float32), precision=lax.Precision.HIGHEST)
    grad_scores = jnp.where(causal[None], grad_mixing * row_scale[None, :, None], 0.0).astype(jnp.bfloat16)
    grad_wide = grad_scores.astype(jnp.float32)
    grad_query = jnp.einsum('hts,shd->thd', grad_wide, key_rows.astype(jnp.float32), precision=lax.Precision.HIGHEST)
    grad_query = grad_query + row_scale[:, None, None] * jnp.einsum('the,hde->thd', cot_wide, state_in, precision=lax.Precision.HIGHEST)
    grad_key = jnp.einsum('hts,thd->shd', grad_wide, query.astype(jnp.float32), precision=lax.Precision.HIGHEST)
    grad_value = jnp.einsum('hts,the->she', mixing.astype(jnp.float32), cot_wide, precision=lax.Precision.HIGHEST)
    if suffix_in is not None:
        grad_key = grad_key + jnp.einsum('she,hde->shd', value_rows.astype(jnp.float32), suffix_in, precision=lax.Precision.HIGHEST)
        grad_value = grad_value + jnp.einsum('shd,hde->she', key_rows.astype(jnp.float32), suffix_in, precision=lax.Precision.HIGHEST)
    return (grad_query.astype(jnp.bfloat16), grad_key.astype(jnp.bfloat16), grad_value.astype(jnp.bfloat16))

def reference(prompt_query, prompt_key, prompt_value, prompt_cotangent, reply_query, reply_key, reply_value, reply_cotangent, reply_weight, reply_length):
    blocks = P_SIZE // PROMPT_DEV

    def split_blocks(array):
        return array.reshape(blocks, PROMPT_DEV, H, E)
    prompt_inputs = (split_blocks(prompt_query), split_blocks(prompt_key), split_blocks(prompt_value), split_blocks(prompt_cotangent), jnp.arange(blocks, dtype=jnp.int32))

    def prompt_forward(running, inputs):
        query, key_rows, value_rows, cotangent, block_number = inputs
        row_scale = position_scale(block_number * PROMPT_DEV, PROMPT_DEV)
        mixing, inner_sum = forward_pieces(query, key_rows, value_rows, row_scale)
        output = inner_sum + carried_term(query, running, row_scale)
        return (running + local_state(key_rows, value_rows), (output.astype(jnp.bfloat16), running))
    zero_state = jnp.zeros((H, E, E), jnp.float32)
    final_state, (prompt_blocks, before_states) = lax.scan(prompt_forward, zero_state, prompt_inputs)
    reply_scale = position_scale(P_SIZE, L)

    def reply_pass(running, inputs):
        query, key_rows, value_rows, cotangent, weight_value, length_value = inputs
        live_mask = (jnp.arange(L, dtype=jnp.int32) < length_value)[:, None, None]
        mixing, inner_sum = forward_pieces(query, key_rows, value_rows, reply_scale)
        output = jnp.where(live_mask, inner_sum + carried_term(query, final_state, reply_scale), 0.0).astype(jnp.bfloat16)
        weighted = (weight_value * jnp.where(live_mask, cotangent.astype(jnp.float32), 0.0)).astype(jnp.bfloat16)
        grads = backward_pieces(query, key_rows, value_rows, weighted, mixing, reply_scale, final_state, None)
        return (running + local_moment(query, weighted, reply_scale), (output,) + grads)
    reply_moment, reply_results = lax.scan(reply_pass, zero_state, (reply_query, reply_key, reply_value, reply_cotangent, reply_weight, reply_length))

    def prompt_backward(running, inputs):
        query, key_rows, value_rows, cotangent, block_number, state_in = inputs
        row_scale = position_scale(block_number * PROMPT_DEV, PROMPT_DEV)
        mixing, inner_sum = forward_pieces(query, key_rows, value_rows, row_scale)
        grads = backward_pieces(query, key_rows, value_rows, cotangent, mixing, row_scale, state_in, running)
        return (running + local_moment(query, cotangent, row_scale), grads)
    spent_moment, prompt_grads = lax.scan(prompt_backward, reply_moment, prompt_inputs + (before_states,), reverse=True)

    def join_blocks(array):
        return array.reshape(P_SIZE, H, E)
    return (join_blocks(prompt_blocks), reply_results[0], join_blocks(prompt_grads[0]), join_blocks(prompt_grads[1]), join_blocks(prompt_grads[2]), reply_results[1], reply_results[2], reply_results[3])
```

```python
import jax
import jax.numpy as jnp
from jax import lax
from jax.experimental import pallas as pl
from jax.experimental.pallas import tpu as pltpu
from jax.sharding import PartitionSpec as P

MESH = pl.DeviceIdType.MESH
F32 = jnp.float32
BF16 = jnp.bfloat16
NY, NX, NZ, NC = 8, 4, 8, 2
E = 128
ROWS = 1024
PROMPT_HEADS = 4
REPLY_HEADS = 2
BLK = 256
SL = E // NY

NN = (((1,), (0,)), ((), ()))
NT = (((1,), (1,)), ((), ()))
TN = (((0,), (0,)), ((), ()))


def dot(a, b, dims):
    return lax.dot_general(a, b, dims, preferred_element_type=F32)


def scale_rows(x, first, heads):
    s = lax.broadcasted_iota(jnp.int32, x.shape, 0)
    pos = (first + s // heads).astype(F32)
    return (x.astype(F32) * lax.rsqrt(float(E) * (pos + 1.0))).astype(BF16)


def by_head(x, heads):
    period = lax.broadcasted_iota(jnp.int32, (16, E), 0) & (heads - 1)
    tiles = x.reshape(ROWS // 16, 16, E)
    parts = []
    for h in range(heads):
        keep = jnp.where(period == h, 1.0, 0.0).astype(BF16)
        parts.append((tiles * keep[None]).reshape(ROWS, E))
    return jnp.concatenate(parts, axis=1)


def reply_weighted(c, weight, length):
    s = lax.broadcasted_iota(jnp.int32, c.shape, 0)
    live = (s // REPLY_HEADS) < length
    return (weight * jnp.where(live, c.astype(F32), 0.0)).astype(BF16)


def wait_bytes(view, sem):
    pltpu.make_async_copy(view, view, sem).wait()


def exchange_kernel(
    pq, pk, pv, pc, rq, rc, weight, length,
    bef_out, aft_out, fin_out,
    loc, wl, xr, yt, yr, ys, yb, xs, st, zf, fin, wr, wz, wzr,
    x_send, x_recv, y_send, y_recv, b_send, b_recv, s_send, s_recv,
    z_send, z_recv, f_send, f_recv, w_send, w_recv, v_send, v_recv,
):
    y = lax.axis_index("ctx")
    x = lax.axis_index("head")
    r = lax.axis_index("resp")
    z = r // 2
    c = r % 2
    fx = 2 * c + x // 2
    wc = x // 2
    wx = 2 * (x % 2)
    loops_back = fx == x

    barrier = pltpu.get_barrier_semaphore()

    def signal(device):
        pl.semaphore_signal(barrier, inc=1, device_id=device, device_id_type=MESH)

    def is_me(device):
        return (device[0] == y) & (device[1] == x) & (device[2] == r)

    def row_peer(d):
        return (y, (x + d) % NX, r)

    def col_peer(d):
        return ((y + d) % NY, x, r)

    def z_peer(d):
        return (y, x, 2 * ((z + d) % NZ) + c)

    def fin_peer(n):
        return (n // 2, fx, 2 * z + n % 2)

    def w_peer(n):
        return (n // 2, wx + n % 2, 2 * z + wc)

    @pl.loop(1, NX)
    def _(d):
        signal(row_peer(d))

    @pl.loop(1, NY)
    def _(d):
        signal(col_peer(d))
        signal(z_peer(d))

    @pl.loop(0, 16)
    def _(n):
        one, two = fin_peer(n), w_peer(n)

        @pl.when(jnp.logical_not(is_me(one)))
        def _():
            signal(one)

        @pl.when(jnp.logical_not(is_me(two)))
        def _():
            signal(two)

    block = y * NX + x
    wide = dot(pk[...], by_head(pv[...], PROMPT_HEADS), TN)
    for h in range(PROMPT_HEADS):
        loc[0, h] = wide[:, h * E:(h + 1) * E]

    @pl.when(loops_back)
    def _():
        pl.semaphore_wait(barrier, 3 + 7 + 7 + 30)

    @pl.when(jnp.logical_not(loops_back))
    def _():
        pl.semaphore_wait(barrier, 3 + 7 + 7 + 32)

    def x_copy(k, d):
        peer = row_peer(d)
        return pltpu.make_async_remote_copy(
            src_ref=loc.at[k, peer[1]], dst_ref=xr.at[k, x],
            send_sem=x_send.at[k], recv_sem=x_recv.at[k],
            device_id=peer, device_id_type=MESH)

    def x_start(k):
        @pl.loop(1, NX)
        def _(d):
            x_copy(k, d).start()
        xr[k, x] = loc[k, x]

    x_start(0)

    weighted = reply_weighted(rc[...], weight[0], length[0])
    rqs = scale_rows(rq[...], NY * NX * (ROWS // PROMPT_HEADS), REPLY_HEADS)
    wide = dot(rqs, by_head(weighted, REPLY_HEADS), TN)
    for i in range(REPLY_HEADS):
        wl[i] = wide[:, i * E:(i + 1) * E].reshape(NY, SL, E)

    @pl.loop(0, 16)
    def _(n):
        peer = w_peer(n)

        @pl.when(jnp.logical_not(is_me(peer)))
        def _():
            pltpu.make_async_remote_copy(
                src_ref=wl.at[n % 2, n // 2], dst_ref=wr.at[2 * y + c],
                send_sem=w_send, recv_sem=w_recv,
                device_id=peer, device_id_type=MESH).start()

    @pl.when(loops_back)
    def _():
        wr[2 * y + c] = wl[x % 2, y]

    pqs = scale_rows(pq[...], block * (ROWS // PROMPT_HEADS), PROMPT_HEADS)
    wide = dot(pqs, by_head(pc[...], PROMPT_HEADS), TN)
    for h in range(PROMPT_HEADS):
        loc[1, h] = wide[:, h * E:(h + 1) * E]
    x_start(1)

    def y_start(k):
        wait_bytes(xr.at[k, pl.ds(0, NX - 1)], x_recv.at[k])
        total = (xr[k, 0] + xr[k, 1]) + (xr[k, 2] + xr[k, 3])
        yt[k] = total.reshape(NY, SL, E)

        @pl.loop(1, NY)
        def _(d):
            peer = col_peer(d)
            pltpu.make_async_remote_copy(
                src_ref=yt.at[k, peer[0]], dst_ref=yr.at[k, y],
                send_sem=y_send.at[k], recv_sem=y_recv.at[k],
                device_id=peer, device_id_type=MESH).start()
        yr[k, y] = yt[k, y]

    def b_start(k):
        @pl.loop(1, NY)
        def _(d):
            peer = col_peer(d)
            pltpu.make_async_remote_copy(
                src_ref=ys.at[k, peer[0]], dst_ref=yb.at[k, y],
                send_sem=b_send.at[k], recv_sem=b_recv.at[k],
                device_id=peer, device_id_type=MESH).start()
        yb[k, y] = ys[k, y]

    def s_start(k):
        @pl.loop(1, NX)
        def _(d):
            peer = row_peer(d)
            pltpu.make_async_remote_copy(
                src_ref=xs.at[k, peer[1]], dst_ref=st.at[k, x],
                send_sem=s_send.at[k], recv_sem=s_recv.at[k],
                device_id=peer, device_id_type=MESH).start()
        st[k, x] = xs[k, x]

    y_start(0)

    @pl.when(loops_back)
    def _():
        wait_bytes(wr.at[pl.ds(0, 15)], w_recv)

    @pl.when(jnp.logical_not(loops_back))
    def _():
        wait_bytes(wr, w_recv)

    for n in range(NY):
        wz[n] = wr[2 * n] + wr[2 * n + 1]

    @pl.loop(1, NZ)
    def _(d):
        to = (z + d) % NZ
        pltpu.make_async_remote_copy(
            src_ref=wz.at[to], dst_ref=wzr.at[z],
            send_sem=v_send, recv_sem=v_recv,
            device_id=(y, x, 2 * to + c), device_id_type=MESH).start()
    wzr[z] = wz[z]

    wait_bytes(yr.at[0, pl.ds(0, NY - 1)], y_recv.at[0])
    running = jnp.zeros((SL, E), F32)
    for n in range(NY):
        ys[0, n] = running
        running = running + yr[0, n]
    zf[z] = running
    b_start(0)

    @pl.loop(1, NZ)
    def _(d):
        pltpu.make_async_remote_copy(
            src_ref=zf.at[z], dst_ref=zf.at[z],
            send_sem=z_send, recv_sem=z_recv,
            device_id=z_peer(d), device_id_type=MESH).start()

    y_start(1)

    wait_bytes(yb.at[0, pl.ds(0, NY - 1)], b_recv.at[0])
    running = yb[0].reshape(E, E)
    for n in range(NX):
        xs[0, n] = running
        if n < NX - 1:
            running = running + xr[0, n]
    s_start(0)

    wait_bytes(wzr.at[pl.ds(0, NZ - 1)], v_recv)
    wait_bytes(yr.at[1, pl.ds(0, NY - 1)], y_recv.at[1])
    running = wzr[0]
    for n in range(1, NZ):
        running = running + wzr[n]
    for n in reversed(range(NY)):
        ys[1, n] = running
        if n > 0:
            running = running + yr[1, n]
    b_start(1)

    wait_bytes(zf.at[pl.ds(0, NZ - 1)], z_recv)

    @pl.loop(0, 16)
    def _(n):
        peer = fin_peer(n)

        @pl.when(jnp.logical_not(is_me(peer)))
        def _():
            pltpu.make_async_remote_copy(
                src_ref=zf.at[n // 2], dst_ref=fin.at[(x % 2) * NY + y],
                send_sem=f_send, recv_sem=f_recv,
                device_id=peer, device_id_type=MESH).start()

    @pl.when(loops_back)
    def _():
        fin[(x % 2) * NY + y] = zf[y]

    wait_bytes(yb.at[1, pl.ds(0, NY - 1)], b_recv.at[1])
    running = yb[1].reshape(E, E)
    for n in reversed(range(NX)):
        xs[1, n] = running
        if n > 0:
            running = running + xr[1, n]
    s_start(1)

    wait_bytes(st.at[0, pl.ds(0, NX - 1)], s_recv.at[0])
    bef_out[...] = st[0].reshape(NX * E, E).astype(BF16)

    @pl.when(loops_back)
    def _():
        wait_bytes(fin.at[pl.ds(0, 15)], f_recv)

    @pl.when(jnp.logical_not(loops_back))
    def _():
        wait_bytes(fin, f_recv)

    fin_out[...] = fin[...].reshape(REPLY_HEADS * E, E).astype(BF16)
    wait_bytes(st.at[1, pl.ds(0, NX - 1)], s_recv.at[1])
    aft_out[...] = st[1].reshape(NX * E, E).astype(BF16)

    for k in range(2):
        wait_bytes(loc.at[k, pl.ds(0, NX - 1)], x_send.at[k])
        wait_bytes(yt.at[k, pl.ds(0, NY - 1)], y_send.at[k])
        wait_bytes(ys.at[k, pl.ds(0, NY - 1)], b_send.at[k])
        wait_bytes(xs.at[k, pl.ds(0, NX - 1)], s_send.at[k])
    wait_bytes(zf.at[pl.ds(0, NZ - 1)], z_send)
    wait_bytes(wz.at[pl.ds(0, NZ - 1)], v_send)

    @pl.when(loops_back)
    def _():
        wait_bytes(fin.at[pl.ds(0, 15)], f_send)
        wait_bytes(wr.at[pl.ds(0, 15)], w_send)

    @pl.when(jnp.logical_not(loops_back))
    def _():
        wait_bytes(fin, f_send)
        wait_bytes(wr, w_send)


def exchange(pq, pk, pv, pc, rq, rc, weight, length):
    vmem = pl.BlockSpec(memory_space=pltpu.VMEM)
    smem = pl.BlockSpec(memory_space=pltpu.SMEM)
    dma = pltpu.SemaphoreType.DMA
    state = (E, E)
    return pl.pallas_call(
        exchange_kernel,
        out_shape=(
            jax.ShapeDtypeStruct((PROMPT_HEADS * E, E), BF16),
            jax.ShapeDtypeStruct((PROMPT_HEADS * E, E), BF16),
            jax.ShapeDtypeStruct((REPLY_HEADS * E, E), BF16),
        ),
        in_specs=[vmem] * 6 + [smem] * 2,
        out_specs=(vmem, vmem, vmem),
        scratch_shapes=[
            pltpu.VMEM((2, NX) + state, F32),
            pltpu.VMEM((2, NY, SL, E), F32),
            pltpu.VMEM((2, NX) + state, F32),
            pltpu.VMEM((2, NY, SL, E), F32),
            pltpu.VMEM((2, NY, SL, E), F32),
            pltpu.VMEM((2, NY, SL, E), F32),
            pltpu.VMEM((2, NY, SL, E), F32),
            pltpu.VMEM((2, NX) + state, F32),
            pltpu.VMEM((2, NX) + state, F32),
            pltpu.VMEM((NZ, SL, E), F32),
            pltpu.VMEM((16, SL, E), F32),
            pltpu.VMEM((16, SL, E), F32),
            pltpu.VMEM((NZ, SL, E), F32),
            pltpu.VMEM((NZ, SL, E), F32),
            dma((2,)), dma((2,)), dma((2,)), dma((2,)),
            dma((2,)), dma((2,)), dma((2,)), dma((2,)),
            dma, dma, dma, dma, dma, dma, dma, dma,
        ],
        compiler_params=pltpu.CompilerParams(
            collective_id=0, has_side_effects=True),
        name="exchange",
    )(pq, pk, pv, pc, rq, rc, weight, length)


def pair_masks(heads):
    a = lax.broadcasted_iota(jnp.int32, (BLK, BLK), 0)
    b = lax.broadcasted_iota(jnp.int32, (BLK, BLK), 1)
    same = ((a ^ b) & (heads - 1)) == 0
    off = jnp.where(same, 1.0, 0.0)
    diag = jnp.where(a >= b, off, 0.0)
    return off.astype(BF16), diag.astype(BF16)


def mixings(left, right, heads, dest):
    off, diag = pair_masks(heads)
    for i in range(ROWS // BLK):
        rows = pl.ds(i * BLK, BLK)
        for j in range(i + 1):
            cols = pl.ds(j * BLK, BLK)
            part = dot(left[i * BLK:(i + 1) * BLK], right[j * BLK:(j + 1) * BLK], NT)
            dest[rows, cols] = part.astype(BF16) * (diag if i == j else off)


def finish_kernel(
    pq, pk, pv, pc, rq, rk, rv, rc, bef, aft, fin, weight, length,
    po, pdq, pdk, pdv, ro, rdq, rdk, rdv,
    mix, gmix, lin,
):
    block = lax.axis_index("ctx") * NX + lax.axis_index("head")

    def blocks(narrow, wide_out, grad_out, key_out, value_out, q, k, v, cot, live):
        for i in range(ROWS // BLK):
            rows = slice(i * BLK, (i + 1) * BLK)
            upto = slice(0, (i + 1) * BLK)
            onward = slice(i * BLK, ROWS)
            part = dot(mix[rows, upto], v[upto], NN) + lin[0, rows]
            if live is not None:
                s = i * BLK + lax.broadcasted_iota(jnp.int32, (BLK, E), 0)
                part = jnp.where((s // REPLY_HEADS) < live, part, 0.0)
            wide_out[rows] = part.astype(BF16)
            part = dot(gmix[rows, upto], k[upto], NN) + lin[1, rows]
            grad_out[rows] = part.astype(BF16)
            part = dot(gmix[onward, rows], q[onward], TN)
            if narrow:
                part = part + lin[2, rows]
            key_out[rows] = part.astype(BF16)
            part = dot(mix[onward, rows], cot[onward], TN)
            if narrow:
                part = part + lin[3, rows]
            value_out[rows] = part.astype(BF16)

    first = block * (ROWS // PROMPT_HEADS)
    qs = scale_rows(pq[...], first, PROMPT_HEADS)
    cs = scale_rows(pc[...], first, PROMPT_HEADS)
    before = bef[...]
    before_wide = jnp.concatenate(
        [before[h * E:(h + 1) * E] for h in range(PROMPT_HEADS)], axis=1)
    after = aft[...]
    after_wide = jnp.concatenate(
        [after[h * E:(h + 1) * E] for h in range(PROMPT_HEADS)], axis=1)
    lin[0] = dot(by_head(qs, PROMPT_HEADS), before, NN)
    lin[1] = dot(by_head(cs, PROMPT_HEADS), before_wide, NT)
    lin[2] = dot(by_head(pv[...], PROMPT_HEADS), after_wide, NT)
    lin[3] = dot(by_head(pk[...], PROMPT_HEADS), after, NN)
    mixings(qs, pk[...], PROMPT_HEADS, mix)
    mixings(cs, pv[...], PROMPT_HEADS, gmix)
    blocks(True, po, pdq, pdk, pdv, pq, pk, pv, pc, None)

    weighted = reply_weighted(rc[...], weight[0], length[0])
    first = NY * NX * (ROWS // PROMPT_HEADS)
    qs = scale_rows(rq[...], first, REPLY_HEADS)
    cs = scale_rows(weighted, first, REPLY_HEADS)
    final = fin[...]
    final_wide = jnp.concatenate(
        [final[h * E:(h + 1) * E] for h in range(REPLY_HEADS)], axis=1)
    lin[0] = dot(by_head(qs, REPLY_HEADS), final, NN)
    lin[1] = dot(by_head(cs, REPLY_HEADS), final_wide, NT)
    mixings(qs, rk[...], REPLY_HEADS, mix)
    mixings(cs, rv[...], REPLY_HEADS, gmix)
    blocks(False, ro, rdq, rdk, rdv, rq, rk, rv, weighted, length[0])


def finish(pq, pk, pv, pc, rq, rk, rv, rc, bef, aft, fin, weight, length):
    vmem = pl.BlockSpec(memory_space=pltpu.VMEM)
    smem = pl.BlockSpec(memory_space=pltpu.SMEM)
    return pl.pallas_call(
        finish_kernel,
        out_shape=tuple([jax.ShapeDtypeStruct((ROWS, E), BF16)] * 8),
        in_specs=[vmem] * 11 + [smem] * 2,
        out_specs=tuple([vmem] * 8),
        scratch_shapes=[
            pltpu.VMEM((ROWS, ROWS), BF16),
            pltpu.VMEM((ROWS, ROWS), BF16),
            pltpu.VMEM((4, ROWS, E), F32),
        ],
        name="finish",
    )(pq, pk, pv, pc, rq, rk, rv, rc, bef, aft, fin, weight, length)


def shards(
    prompt_query, prompt_key, prompt_value, prompt_cotangent,
    reply_query, reply_key, reply_value, reply_cotangent,
    reply_weight, reply_length,
):
    prompt_shape = prompt_query.shape
    reply_shape = reply_query.shape
    pq, pk, pv, pc, rq, rk, rv, rc = [
        a.reshape(ROWS, E)
        for a in (prompt_query, prompt_key, prompt_value, prompt_cotangent,
                  reply_query, reply_key, reply_value, reply_cotangent)
    ]
    bef, aft, fin = exchange(pq, pk, pv, pc, rq, rc, reply_weight, reply_length)
    po, pdq, pdk, pdv, ro, rdq, rdk, rdv = finish(
        pq, pk, pv, pc, rq, rk, rv, rc, bef, aft, fin, reply_weight, reply_length)
    return (
        po.reshape(prompt_shape), ro.reshape(reply_shape),
        pdq.reshape(prompt_shape), pdk.reshape(prompt_shape), pdv.reshape(prompt_shape),
        rdq.reshape(reply_shape), rdk.reshape(reply_shape), rdv.reshape(reply_shape),
    )


def solution(mesh):
    prompt = P(("ctx", "head"), "resp", None)
    reply = P("resp", None, ("ctx", "head"), None)
    placed = (prompt,) * 4 + (reply,) * 4 + (P("resp"), P("resp"))
    return jax.shard_map(
        shards,
        mesh=mesh,
        in_specs=placed,
        out_specs=(prompt, reply, prompt, prompt, prompt, reply, reply, reply),
        check_vma=False,
    )
```

```python
import jax
import jax.numpy as jnp
from jax import lax
from jax.experimental import pallas as pl
from jax.experimental.pallas import tpu as pltpu
from jax.sharding import PartitionSpec as P

MESH = pl.DeviceIdType.MESH
F32 = jnp.float32
BF16 = jnp.bfloat16
NY, NX, NZ, NC = 8, 4, 8, 2
E = 128
ROWS = 1024
PROMPT_HEADS = 4
REPLY_HEADS = 2
BLK = 256
SL = E // NY

NN = (((1,), (0,)), ((), ()))
NT = (((1,), (1,)), ((), ()))
TN = (((0,), (0,)), ((), ()))


def dot(a, b, dims):
    return lax.dot_general(a, b, dims, preferred_element_type=F32)


def scale_rows(x, first, heads):
    s = lax.broadcasted_iota(jnp.int32, x.shape, 0)
    pos = (first + s // heads).astype(F32)
    return (x.astype(F32) * lax.rsqrt(float(E) * (pos + 1.0))).astype(BF16)


def by_head(x, heads):
    period = lax.broadcasted_iota(jnp.int32, (16, E), 0) & (heads - 1)
    tiles = x.reshape(ROWS // 16, 16, E)
    parts = []
    for h in range(heads):
        keep = jnp.where(period == h, 1.0, 0.0).astype(BF16)
        parts.append((tiles * keep[None]).reshape(ROWS, E))
    return jnp.concatenate(parts, axis=1)


def reply_weighted(c, weight, length):
    s = lax.broadcasted_iota(jnp.int32, c.shape, 0)
    live = (s // REPLY_HEADS) < length
    return (weight * jnp.where(live, c.astype(F32), 0.0)).astype(BF16)


def wait_bytes(view, sem):
    pltpu.make_async_copy(view, view, sem).wait()


def pair_masks(heads):
    a = lax.broadcasted_iota(jnp.int32, (BLK, BLK), 0)
    b = lax.broadcasted_iota(jnp.int32, (BLK, BLK), 1)
    same = ((a ^ b) & (heads - 1)) == 0
    off = jnp.where(same, 1.0, 0.0)
    diag = jnp.where(a >= b, off, 0.0)
    return off.astype(BF16), diag.astype(BF16)


def mixings(left, right, heads, dest):
    off, diag = pair_masks(heads)
    for i in range(ROWS // BLK):
        rows = pl.ds(i * BLK, BLK)
        for j in range(i + 1):
            cols = pl.ds(j * BLK, BLK)
            part = dot(left[i * BLK:(i + 1) * BLK], right[j * BLK:(j + 1) * BLK], NT)
            dest[rows, cols] = part.astype(BF16) * (diag if i == j else off)


def stack_wide(state, heads):
    return jnp.concatenate([state[h * E:(h + 1) * E] for h in range(heads)], axis=1)


def exchange_kernel(
    pq_in, pk_in, pv_in, pc_in, rq_in, rk_in, rv_in, rc_in, weight, length,
    po_out, ro_out, pdq_out, rdq_out, rdk_out, rdv_out, pdk_out, pdv_out, aft_out,
    pq, pk, pv, pc, rq, rk, rv, rc,
    po, ro, pdq, rdq, rdk, rdv, pdk, pdv, aft,
    pqs, pcs, rqs, rcs, rw, mix, gmix, part,
    loc, wl, xr, yt, yr, ys, yb, xs, st, zf, fin, wr, wz, wzr,
    in_sem, out_sem,
    x_send, x_recv, y_send, y_recv, b_send, b_recv, s_send, s_recv,
    z_send, z_recv, f_send, f_recv, w_send, w_recv, v_send, v_recv,
):
    y = lax.axis_index("ctx")
    x = lax.axis_index("head")
    r = lax.axis_index("resp")
    z = r // 2
    c = r % 2
    fx = 2 * c + x // 2
    wc = x // 2
    wx = 2 * (x % 2)
    loops_back = fx == x

    barrier = pltpu.get_barrier_semaphore()

    loads = [
        pltpu.make_async_copy(src, dst, in_sem.at[n])
        for n, (src, dst) in enumerate((
            (pk_in, pk), (pv_in, pv), (rq_in, rq), (rc_in, rc),
            (pq_in, pq), (pc_in, pc), (rk_in, rk), (rv_in, rv)))
    ]
    for load in loads:
        load.start()

    def save(n, src, dst):
        copy = pltpu.make_async_copy(src, dst, out_sem.at[n])
        copy.start()
        return copy

    def signal(device):
        pl.semaphore_signal(barrier, inc=1, device_id=device, device_id_type=MESH)

    def is_me(device):
        return (device[0] == y) & (device[1] == x) & (device[2] == r)

    def row_peer(d):
        return (y, (x + d) % NX, r)

    def col_peer(d):
        return ((y + d) % NY, x, r)

    def z_peer(d):
        return (y, x, 2 * ((z + d) % NZ) + c)

    def fin_peer(n):
        return (n // 2, fx, 2 * z + n % 2)

    def w_peer(n):
        return (n // 2, wx + n % 2, 2 * z + wc)

    @pl.loop(1, NX)
    def _(d):
        signal(row_peer(d))

    @pl.loop(1, NY)
    def _(d):
        signal(col_peer(d))
        signal(z_peer(d))

    @pl.loop(0, 16)
    def _(n):
        one, two = fin_peer(n), w_peer(n)

        @pl.when(jnp.logical_not(is_me(one)))
        def _():
            signal(one)

        @pl.when(jnp.logical_not(is_me(two)))
        def _():
            signal(two)

    block = y * NX + x
    prompt_first = block * (ROWS // PROMPT_HEADS)
    reply_first = NY * NX * (ROWS // PROMPT_HEADS)
    loads[0].wait()
    loads[1].wait()
    wide = dot(pk[...], by_head(pv[...], PROMPT_HEADS), TN)
    for h in range(PROMPT_HEADS):
        loc[0, h] = wide[:, h * E:(h + 1) * E]

    @pl.when(loops_back)
    def _():
        pl.semaphore_wait(barrier, 3 + 7 + 7 + 30)

    @pl.when(jnp.logical_not(loops_back))
    def _():
        pl.semaphore_wait(barrier, 3 + 7 + 7 + 32)

    def x_start(k):
        @pl.loop(1, NX)
        def _(d):
            peer = row_peer(d)
            pltpu.make_async_remote_copy(
                src_ref=loc.at[k, peer[1]], dst_ref=xr.at[k, x],
                send_sem=x_send.at[k], recv_sem=x_recv.at[k],
                device_id=peer, device_id_type=MESH).start()
        xr[k, x] = loc[k, x]

    x_start(0)

    loads[2].wait()
    loads[3].wait()
    rw[...] = reply_weighted(rc[...], weight[0], length[0])
    rqs[...] = scale_rows(rq[...], reply_first, REPLY_HEADS)
    wide = dot(rqs[...], by_head(rw[...], REPLY_HEADS), TN)
    for i in range(REPLY_HEADS):
        wl[i] = wide[:, i * E:(i + 1) * E].reshape(NY, SL, E)

    @pl.loop(0, 16)
    def _(n):
        peer = w_peer(n)

        @pl.when(jnp.logical_not(is_me(peer)))
        def _():
            pltpu.make_async_remote_copy(
                src_ref=wl.at[n % 2, n // 2], dst_ref=wr.at[2 * y + c],
                send_sem=w_send, recv_sem=w_recv,
                device_id=peer, device_id_type=MESH).start()

    @pl.when(loops_back)
    def _():
        wr[2 * y + c] = wl[x % 2, y]

    loads[4].wait()
    loads[5].wait()
    pqs[...] = scale_rows(pq[...], prompt_first, PROMPT_HEADS)
    wide = dot(pqs[...], by_head(pc[...], PROMPT_HEADS), TN)
    for h in range(PROMPT_HEADS):
        loc[1, h] = wide[:, h * E:(h + 1) * E]
    x_start(1)

    def y_start(k):
        wait_bytes(xr.at[k, pl.ds(0, NX - 1)], x_recv.at[k])
        total = (xr[k, 0] + xr[k, 1]) + (xr[k, 2] + xr[k, 3])
        yt[k] = total.reshape(NY, SL, E)

        @pl.loop(1, NY)
        def _(d):
            peer = col_peer(d)
            pltpu.make_async_remote_copy(
                src_ref=yt.at[k, peer[0]], dst_ref=yr.at[k, y],
                send_sem=y_send.at[k], recv_sem=y_recv.at[k],
                device_id=peer, device_id_type=MESH).start()
        yr[k, y] = yt[k, y]

    def b_start(k):
        @pl.loop(1, NY)
        def _(d):
            peer = col_peer(d)
            pltpu.make_async_remote_copy(
                src_ref=ys.at[k, peer[0]], dst_ref=yb.at[k, y],
                send_sem=b_send.at[k], recv_sem=b_recv.at[k],
                device_id=peer, device_id_type=MESH).start()
        yb[k, y] = ys[k, y]

    def s_start(k):
        @pl.loop(1, NX)
        def _(d):
            peer = row_peer(d)
            pltpu.make_async_remote_copy(
                src_ref=xs.at[k, peer[1]], dst_ref=st.at[k, x],
                send_sem=s_send.at[k], recv_sem=s_recv.at[k],
                device_id=peer, device_id_type=MESH).start()
        st[k, x] = xs[k, x]

    blocks = [(slice(i * BLK, (i + 1) * BLK), slice(0, (i + 1) * BLK), slice(i * BLK, ROWS))
              for i in range(ROWS // BLK)]

    pcs[...] = scale_rows(pc[...], prompt_first, PROMPT_HEADS)
    mixings(pqs, pk, PROMPT_HEADS, mix)
    mixings(pcs, pv, PROMPT_HEADS, gmix)

    y_start(0)

    @pl.when(loops_back)
    def _():
        wait_bytes(wr.at[pl.ds(0, 15)], w_recv)

    @pl.when(jnp.logical_not(loops_back))
    def _():
        wait_bytes(wr, w_recv)

    for n in range(NY):
        wz[n] = wr[2 * n] + wr[2 * n + 1]

    @pl.loop(1, NZ)
    def _(d):
        to = (z + d) % NZ
        pltpu.make_async_remote_copy(
            src_ref=wz.at[to], dst_ref=wzr.at[z],
            send_sem=v_send, recv_sem=v_recv,
            device_id=(y, x, 2 * to + c), device_id_type=MESH).start()
    wzr[z] = wz[z]

    for rows, upto, onward in blocks:
        pdk[rows] = dot(gmix[onward, rows], pq[onward], TN)
        pdv[rows] = dot(mix[onward, rows], pc[onward], TN)
    saves = [save(0, pdk, pdk_out), save(1, pdv, pdv_out)]

    y_start(1)

    wait_bytes(yr.at[0, pl.ds(0, NY - 1)], y_recv.at[0])
    running = jnp.zeros((SL, E), F32)
    for n in range(NY):
        ys[0, n] = running
        running = running + yr[0, n]
    zf[z] = running
    b_start(0)

    @pl.loop(1, NZ)
    def _(d):
        pltpu.make_async_remote_copy(
            src_ref=zf.at[z], dst_ref=zf.at[z],
            send_sem=z_send, recv_sem=z_recv,
            device_id=z_peer(d), device_id_type=MESH).start()

    for rows, upto, onward in blocks:
        part[0, rows] = dot(mix[rows, upto], pv[upto], NN)
        part[1, rows] = dot(gmix[rows, upto], pk[upto], NN)
    loads[6].wait()
    loads[7].wait()
    mixings(rqs, rk, REPLY_HEADS, mix)

    wait_bytes(wzr.at[pl.ds(0, NZ - 1)], v_recv)
    wait_bytes(yr.at[1, pl.ds(0, NY - 1)], y_recv.at[1])
    running = wzr[0]
    for n in range(1, NZ):
        running = running + wzr[n]
    for n in reversed(range(NY)):
        ys[1, n] = running
        if n > 0:
            running = running + yr[1, n]
    b_start(1)

    wait_bytes(zf.at[pl.ds(0, NZ - 1)], z_recv)

    @pl.loop(0, 16)
    def _(n):
        peer = fin_peer(n)

        @pl.when(jnp.logical_not(is_me(peer)))
        def _():
            pltpu.make_async_remote_copy(
                src_ref=zf.at[n // 2], dst_ref=fin.at[(x % 2) * NY + y],
                send_sem=f_send, recv_sem=f_recv,
                device_id=peer, device_id_type=MESH).start()

    @pl.when(loops_back)
    def _():
        fin[(x % 2) * NY + y] = zf[y]

    wait_bytes(yb.at[0, pl.ds(0, NY - 1)], b_recv.at[0])
    running = yb[0].reshape(E, E)
    for n in range(NX):
        xs[0, n] = running
        if n < NX - 1:
            running = running + xr[0, n]
    s_start(0)

    rcs[...] = scale_rows(rw[...], reply_first, REPLY_HEADS)
    mixings(rcs, rv, REPLY_HEADS, gmix)
    for rows, upto, onward in blocks:
        rdv[rows] = dot(mix[onward, rows], rw[onward], TN).astype(BF16)
    saves.append(save(2, rdv, rdv_out))

    wait_bytes(yb.at[1, pl.ds(0, NY - 1)], b_recv.at[1])
    running = yb[1].reshape(E, E)
    for n in reversed(range(NX)):
        xs[1, n] = running
        if n > 0:
            running = running + xr[1, n]
    s_start(1)

    for rows, upto, onward in blocks:
        rdk[rows] = dot(gmix[onward, rows], rq[onward], TN).astype(BF16)
    saves.append(save(3, rdk, rdk_out))
    for rows, upto, onward in blocks:
        part[2, rows] = dot(mix[rows, upto], rv[upto], NN)
        part[3, rows] = dot(gmix[rows, upto], rk[upto], NN)

    wait_bytes(st.at[0, pl.ds(0, NX - 1)], s_recv.at[0])
    before = st[0].reshape(NX * E, E).astype(BF16)
    po[...] = (part[0] + dot(by_head(pqs[...], PROMPT_HEADS), before, NN)).astype(BF16)
    saves.append(save(4, po, po_out))
    wide = stack_wide(before, PROMPT_HEADS)
    pdq[...] = (part[1] + dot(by_head(pcs[...], PROMPT_HEADS), wide, NT)).astype(BF16)
    saves.append(save(5, pdq, pdq_out))

    @pl.when(loops_back)
    def _():
        wait_bytes(fin.at[pl.ds(0, 15)], f_recv)

    @pl.when(jnp.logical_not(loops_back))
    def _():
        wait_bytes(fin, f_recv)

    final = fin[...].reshape(REPLY_HEADS * E, E).astype(BF16)
    out = part[2] + dot(by_head(rqs[...], REPLY_HEADS), final, NN)
    s = lax.broadcasted_iota(jnp.int32, (ROWS, E), 0)
    ro[...] = jnp.where((s // REPLY_HEADS) < length[0], out, 0.0).astype(BF16)
    saves.append(save(6, ro, ro_out))
    wide = stack_wide(final, REPLY_HEADS)
    rdq[...] = (part[3] + dot(by_head(rcs[...], REPLY_HEADS), wide, NT)).astype(BF16)
    saves.append(save(7, rdq, rdq_out))

    wait_bytes(st.at[1, pl.ds(0, NX - 1)], s_recv.at[1])
    aft[...] = st[1].reshape(NX * E, E).astype(BF16)
    saves.append(save(8, aft, aft_out))

    for k in range(2):
        wait_bytes(loc.at[k, pl.ds(0, NX - 1)], x_send.at[k])
        wait_bytes(yt.at[k, pl.ds(0, NY - 1)], y_send.at[k])
        wait_bytes(ys.at[k, pl.ds(0, NY - 1)], b_send.at[k])
        wait_bytes(xs.at[k, pl.ds(0, NX - 1)], s_send.at[k])
    wait_bytes(zf.at[pl.ds(0, NZ - 1)], z_send)
    wait_bytes(wz.at[pl.ds(0, NZ - 1)], v_send)

    @pl.when(loops_back)
    def _():
        wait_bytes(fin.at[pl.ds(0, 15)], f_send)
        wait_bytes(wr.at[pl.ds(0, 15)], w_send)

    @pl.when(jnp.logical_not(loops_back))
    def _():
        wait_bytes(fin, f_send)
        wait_bytes(wr, w_send)

    for copy in saves:
        copy.wait()


def exchange(*args):
    whole = pl.BlockSpec(memory_space=pl.ANY)
    smem = pl.BlockSpec(memory_space=pltpu.SMEM)
    dma = pltpu.SemaphoreType.DMA
    state = (E, E)
    narrow = pltpu.VMEM((ROWS, E), BF16)
    wide = pltpu.VMEM((ROWS, E), F32)
    slices = pltpu.VMEM((2, NY, SL, E), F32)
    return pl.pallas_call(
        exchange_kernel,
        out_shape=tuple(
            [jax.ShapeDtypeStruct((ROWS, E), BF16)] * 6
            + [jax.ShapeDtypeStruct((ROWS, E), F32)] * 2
            + [jax.ShapeDtypeStruct((PROMPT_HEADS * E, E), BF16)]),
        in_specs=[whole] * 8 + [smem] * 2,
        out_specs=tuple([whole] * 9),
        scratch_shapes=[narrow] * 14 + [wide] * 2 + [
            pltpu.VMEM((PROMPT_HEADS * E, E), BF16),
        ] + [narrow] * 5 + [
            pltpu.VMEM((ROWS, ROWS), BF16),
            pltpu.VMEM((ROWS, ROWS), BF16),
            pltpu.VMEM((4, ROWS, E), F32),
            pltpu.VMEM((2, NX) + state, F32),
            slices,
            pltpu.VMEM((2, NX) + state, F32),
            slices, slices, slices, slices,
            pltpu.VMEM((2, NX) + state, F32),
            pltpu.VMEM((2, NX) + state, F32),
            pltpu.VMEM((NZ, SL, E), F32),
            pltpu.VMEM((16, SL, E), F32),
            pltpu.VMEM((16, SL, E), F32),
            pltpu.VMEM((NZ, SL, E), F32),
            pltpu.VMEM((NZ, SL, E), F32),
            dma((8,)), dma((9,)),
            dma((2,)), dma((2,)), dma((2,)), dma((2,)),
            dma((2,)), dma((2,)), dma((2,)), dma((2,)),
            dma, dma, dma, dma, dma, dma, dma, dma,
        ],
        compiler_params=pltpu.CompilerParams(
            collective_id=0, has_side_effects=True),
        name="exchange",
    )(*args)


def finish_kernel(
    po_in, ro_in, pdq_in, rdq_in, rdk_in, rdv_in, pdk_in, pdv_in, aft_in, pk_in, pv_in,
    po_out, ro_out, pdq_out, rdq_out, rdk_out, rdv_out, pdk_out, pdv_out,
    po, ro, pdq, rdq, rdk, rdv, kpart, vpart, aft, pk, pv, pdk, pdv, in_sem, out_sem,
):
    ins = (aft_in, pv_in, pdk_in, pk_in, pdv_in, po_in, ro_in, pdq_in, rdq_in, rdk_in, rdv_in)
    held = (aft, pv, kpart, pk, vpart, po, ro, pdq, rdq, rdk, rdv)
    outs = (po_out, ro_out, pdq_out, rdq_out, rdk_out, rdv_out)
    loads = [pltpu.make_async_copy(src, dst, in_sem.at[n])
             for n, (src, dst) in enumerate(zip(ins, held))]
    for load in loads:
        load.start()
    saves = []

    def save(src, dst):
        copy = pltpu.make_async_copy(src, dst, out_sem.at[len(saves)])
        copy.start()
        saves.append(copy)

    loads[0].wait()
    loads[1].wait()
    wide = stack_wide(aft[...], PROMPT_HEADS)
    grad = dot(by_head(pv[...], PROMPT_HEADS), wide, NT)
    loads[2].wait()
    pdk[...] = (kpart[...] + grad).astype(BF16)
    save(pdk, pdk_out)
    loads[3].wait()
    grad = dot(by_head(pk[...], PROMPT_HEADS), aft[...], NN)
    loads[4].wait()
    pdv[...] = (vpart[...] + grad).astype(BF16)
    save(pdv, pdv_out)
    for n in range(6):
        loads[5 + n].wait()
        save(held[5 + n], outs[n])
    for copy in saves:
        copy.wait()


def finish(*args):
    whole = pl.BlockSpec(memory_space=pl.ANY)
    narrow = pltpu.VMEM((ROWS, E), BF16)
    wide = pltpu.VMEM((ROWS, E), F32)
    return pl.pallas_call(
        finish_kernel,
        out_shape=tuple([jax.ShapeDtypeStruct((ROWS, E), BF16)] * 8),
        in_specs=[whole] * 11,
        out_specs=tuple([whole] * 8),
        scratch_shapes=[narrow] * 6 + [wide] * 2 + [
            pltpu.VMEM((PROMPT_HEADS * E, E), BF16)] + [narrow] * 4 + [
            pltpu.SemaphoreType.DMA((11,)), pltpu.SemaphoreType.DMA((8,))],
        name="finish",
    )(*args)


def shards(
    prompt_query, prompt_key, prompt_value, prompt_cotangent,
    reply_query, reply_key, reply_value, reply_cotangent,
    reply_weight, reply_length,
):
    prompt_shape = prompt_query.shape
    reply_shape = reply_query.shape
    pq, pk, pv, pc, rq, rk, rv, rc = [
        a.reshape(ROWS, E)
        for a in (prompt_query, prompt_key, prompt_value, prompt_cotangent,
                  reply_query, reply_key, reply_value, reply_cotangent)
    ]
    parts = exchange(pq, pk, pv, pc, rq, rk, rv, rc, reply_weight, reply_length)
    po, ro, pdq, rdq, rdk, rdv, pdk, pdv = finish(*parts, pk, pv)
    return (
        po.reshape(prompt_shape), ro.reshape(reply_shape),
        pdq.reshape(prompt_shape), pdk.reshape(prompt_shape), pdv.reshape(prompt_shape),
        rdq.reshape(reply_shape), rdk.reshape(reply_shape), rdv.reshape(reply_shape),
    )


def solution(mesh):
    prompt = P(("ctx", "head"), "resp", None)
    reply = P("resp", None, ("ctx", "head"), None)
    placed = (prompt,) * 4 + (reply,) * 4 + (P("resp"), P("resp"))
    return jax.shard_map(
        shards,
        mesh=mesh,
        in_specs=placed,
        out_specs=(prompt, reply, prompt, prompt, prompt, reply, reply, reply),
        check_vma=False,
    )
```

```python
import jax
import jax.numpy as jnp
from jax import lax
from jax.experimental import pallas as pl
from jax.experimental.pallas import tpu as pltpu
from jax.sharding import PartitionSpec as P

MESH = pl.DeviceIdType.MESH
F32 = jnp.float32
BF16 = jnp.bfloat16
NY, NX, NZ, NC = 8, 4, 8, 2
E = 128
ROWS = 1024
PROMPT_HEADS = 4
REPLY_HEADS = 2
BLK = 256
SL = E // NY
FAR = [4, 3, 5, 2, 6, 1, 7, 0]
NEAR = [0, 1, 7, 2, 6, 3, 5, 4]

NN = (((1,), (0,)), ((), ()))
NT = (((1,), (1,)), ((), ()))
TN = (((0,), (0,)), ((), ()))


def dot(a, b, dims):
    return lax.dot_general(a, b, dims, preferred_element_type=F32)


def scale_rows(x, first, heads):
    s = lax.broadcasted_iota(jnp.int32, x.shape, 0)
    pos = (first + s // heads).astype(F32)
    return (x.astype(F32) * lax.rsqrt(float(E) * (pos + 1.0))).astype(BF16)


def by_head(x, heads):
    period = lax.broadcasted_iota(jnp.int32, (16, E), 0) & (heads - 1)
    tiles = x.reshape(ROWS // 16, 16, E)
    parts = []
    for h in range(heads):
        keep = jnp.where(period == h, 1.0, 0.0).astype(BF16)
        parts.append((tiles * keep[None]).reshape(ROWS, E))
    return jnp.concatenate(parts, axis=1)


def reply_weighted(c, weight, length):
    s = lax.broadcasted_iota(jnp.int32, c.shape, 0)
    live = (s // REPLY_HEADS) < length
    return (weight * jnp.where(live, c.astype(F32), 0.0)).astype(BF16)


def wait_bytes(view, sem):
    pltpu.make_async_copy(view, view, sem).wait()


def pair_masks(heads):
    a = lax.broadcasted_iota(jnp.int32, (BLK, BLK), 0)
    b = lax.broadcasted_iota(jnp.int32, (BLK, BLK), 1)
    same = ((a ^ b) & (heads - 1)) == 0
    off = jnp.where(same, 1.0, 0.0)
    diag = jnp.where(a >= b, off, 0.0)
    return off.astype(BF16), diag.astype(BF16)


def mixings(left, right, heads, dest):
    off, diag = pair_masks(heads)
    for i in range(ROWS // BLK):
        rows = pl.ds(i * BLK, BLK)
        for j in range(i + 1):
            cols = pl.ds(j * BLK, BLK)
            part = dot(left[i * BLK:(i + 1) * BLK], right[j * BLK:(j + 1) * BLK], NT)
            dest[rows, cols] = part.astype(BF16) * (diag if i == j else off)


def stack_wide(state, heads):
    return jnp.concatenate([state[h * E:(h + 1) * E] for h in range(heads)], axis=1)


def exchange_kernel(
    pq_in, pk_in, pv_in, pc_in, rq_in, rk_in, rv_in, rc_in, weight, length,
    po_out, ro_out, pdq_out, rdq_out, rdk_out, rdv_out, pdk_out, pdv_out, aft_out,
    pq, pk, pv, pc, rq, rk, rv, rc,
    po, ro, pdq, rdq, rdk, rdv, pdk, pdv, aft, bef,
    pqs, pcs, rqs, rcs, rw, mix, gmix, part,
    raw, loc, xr, yt, yr, ys, yb, xs, st, tot, fin, wl, wy, wq, wt, wf,
    in_sem, out_sem,
    x_send, x_recv, y_send, y_recv, b_send, b_recv, s_send, s_recv,
    f_send, f_recv, w_send, w_recv, v_send, v_recv, u_send, u_recv,
):
    y = lax.axis_index("ctx")
    x = lax.axis_index("head")
    r = lax.axis_index("resp")
    z = r // 2
    c = r % 2
    fx = 2 * c + x // 2
    wc = x // 2
    wx = 2 * (x % 2)
    same_column = fx == x
    loops_back = same_column & (z == y)
    gathers = c == wc

    barrier = pltpu.get_barrier_semaphore()

    loads = [
        pltpu.make_async_copy(src, dst, in_sem.at[n])
        for n, (src, dst) in enumerate((
            (pk_in, pk), (pv_in, pv), (rq_in, rq), (rc_in, rc),
            (pq_in, pq), (pc_in, pc), (rk_in, rk), (rv_in, rv)))
    ]
    for load in loads:
        load.start()

    saves = []

    def save(src, dst):
        copy = pltpu.make_async_copy(src, dst, out_sem.at[len(saves)])
        copy.start()
        saves.append(copy)

    def send(src, dst, send_sem, recv_sem, device):
        pltpu.make_async_remote_copy(
            src_ref=src, dst_ref=dst, send_sem=send_sem, recv_sem=recv_sem,
            device_id=device, device_id_type=MESH).start()

    def signal(device):
        pl.semaphore_signal(barrier, inc=1, device_id=device, device_id_type=MESH)

    @pl.loop(1, NX)
    def _(d):
        signal((y, (x + d) % NX, r))

    @pl.loop(1, NY)
    def _(d):
        signal(((y + d) % NY, x, r))

    @pl.loop(1, NZ * NC)
    def _(d):
        signal((y, x, (r + d) % (NZ * NC)))

    block = y * NX + x
    prompt_first = block * (ROWS // PROMPT_HEADS)
    reply_first = NY * NX * (ROWS // PROMPT_HEADS)

    def states(k, left, right):
        wide = dot(left, by_head(right, PROMPT_HEADS), TN)
        for h in range(PROMPT_HEADS):
            raw[h] = wide[:, h * E:(h + 1) * E].reshape(NY, SL, E)
        for p in range(NY):
            row = (y + FAR[p]) % NY
            for h in range(PROMPT_HEADS):
                loc[k, h, p] = raw[h, row]

    def x_start(k):
        for piece in range(NY // 2):
            span = pl.ds(2 * piece, 2)

            @pl.loop(1, NX)
            def _(d):
                to = (x + d) % NX
                send(loc.at[k, to, span], xr.at[k, x, span],
                     x_send.at[k], x_recv.at[k, piece], (y, to, r))
        xr[k, x] = loc[k, x]

    def y_piece(k, piece):
        wait_bytes(xr.at[k, 0, pl.ds(0, 2 * (NX - 1))], x_recv.at[k, piece])
        for p in (2 * piece, 2 * piece + 1):
            yt[k, p] = (xr[k, 0, p] + xr[k, 1, p]) + (xr[k, 2, p] + xr[k, 3, p])
            if FAR[p]:
                send(yt.at[k, p], yr.at[k, y], y_send.at[k], y_recv.at[k],
                     ((y + FAR[p]) % NY, x, r))
            else:
                yr[k, y] = yt[k, p]

    def b_start(k):
        for rel in FAR[:-1]:
            to = (y + rel) % NY
            back = (NY - rel) % NY
            send(ys.at[k, to], yb.at[k, NEAR.index(back)],
                 b_send.at[k], b_recv.at[k, min(back, NY - back) - 1], (to, x, r))
        yb[k, 0] = ys[k, y]

    def s_piece(k, piece):
        first, count = ((0, 3), (3, 2), (5, 2), (7, 1))[piece]
        wait_bytes(yb.at[k, pl.ds(0, 1 if piece == 3 else 2)], b_recv.at[k, piece])
        for q in range(first, first + count):
            p = FAR.index(NEAR[q])
            running = yb[k, q]
            order = range(NX) if k == 0 else range(NX - 1, -1, -1)
            for n in order:
                xs[k, n, q] = running
                running = running + xr[k, n, p]
        span = pl.ds(first, count)

        @pl.loop(1, NX)
        def _(d):
            to = (x + d) % NX
            send(xs.at[k, to, span], st.at[k, x, span],
                 s_send.at[k], s_recv.at[k], (y, to, r))
        for q in range(first, first + count):
            st[k, x, q] = xs[k, x, q]

    def collect(k, dest):
        wait_bytes(st.at[k, pl.ds(0, NX - 1)], s_recv.at[k])
        for q in range(NY):
            row = (y + NEAR[q]) % NY
            for h in range(PROMPT_HEADS):
                dest[h, row] = st[k, h, q].astype(BF16)

    loads[0].wait()
    loads[1].wait()
    states(0, pk[...], pv[...])

    loads[2].wait()
    loads[3].wait()
    rw[...] = reply_weighted(rc[...], weight[0], length[0])
    rqs[...] = scale_rows(rq[...], reply_first, REPLY_HEADS)
    wide = dot(rqs[...], by_head(rw[...], REPLY_HEADS), TN)
    for i in range(REPLY_HEADS):
        moment = wide[:, i * E:(i + 1) * E].reshape(NY, SL, E)
        for n in range(NY):
            wl[n, i] = moment[n]

    pl.semaphore_wait(barrier, NX - 1 + NY - 1 + NZ * NC - 1)
    x_start(0)
    for rel in FAR[:-1]:
        to = (y + rel) % NY
        send(wl.at[to], wy.at[y], w_send, w_recv, (to, x, r))
    wy[y] = wl[y]

    loads[4].wait()
    loads[5].wait()
    pqs[...] = scale_rows(pq[...], prompt_first, PROMPT_HEADS)
    states(1, pqs[...], pc[...])
    x_start(1)

    blocks = [(slice(i * BLK, (i + 1) * BLK), slice(0, (i + 1) * BLK), slice(i * BLK, ROWS))
              for i in range(ROWS // BLK)]

    mixings(pqs, pk, PROMPT_HEADS, mix)

    for piece in range(NY // 2):
        y_piece(0, piece)

    wait_bytes(wy.at[pl.ds(0, NY - 1)], w_recv)

    @pl.loop(0, NZ)
    def _(n):
        to = 2 * n + wc

        @pl.when(to != r)
        def _():
            send(wy.at[n], wq.at[r], v_send, v_recv, (y, x, to))

    @pl.when(gathers)
    def _():
        wq[r] = wy[z]

    for piece in range(NY // 2):
        y_piece(1, piece)

    wait_bytes(yr.at[0, pl.ds(0, NY - 1)], y_recv.at[0])
    running = jnp.zeros((SL, E), F32)
    for n in range(NY):
        ys[0, n] = running
        running = running + yr[0, n]
    tot[...] = running
    b_start(0)

    @pl.loop(0, NZ * NC)
    def _(n):
        to = (2 * z + NZ + n) % (NZ * NC)

        @pl.when(jnp.logical_not(loops_back & (to == r)))
        def _():
            send(tot, fin.at[(x % 2) * NY + y], f_send, f_recv, (z, fx, to))

    @pl.when(loops_back)
    def _():
        fin[(x % 2) * NY + y] = tot[...]

    pcs[...] = scale_rows(pc[...], prompt_first, PROMPT_HEADS)
    mixings(pcs, pv, PROMPT_HEADS, gmix)

    s_piece(0, 0)
    s_piece(0, 1)

    @pl.when(gathers)
    def _():
        wait_bytes(wq.at[pl.ds(0, NZ * NC - 1)], v_recv)
        total = wq[0]
        for n in range(1, NZ * NC):
            total = total + wq[n]
        wt[...] = total

        @pl.loop(0, REPLY_HEADS)
        def _(i):
            @pl.when(wx + i != x)
            def _():
                send(wt.at[i], wf, u_send, u_recv, (y, wx + i, r))

        @pl.when(same_column)
        def _():
            wf[...] = wt[x % 2]

    s_piece(0, 2)
    s_piece(0, 3)

    wait_bytes(yr.at[1, pl.ds(0, NY - 1)], y_recv.at[1])

    @pl.when(jnp.logical_not(same_column))
    def _():
        wait_bytes(wf, u_recv)

    running = wf[...]
    for n in reversed(range(NY)):
        ys[1, n] = running
        running = running + yr[1, n]
    b_start(1)

    for rows, upto, onward in blocks:
        pdk[rows] = dot(gmix[onward, rows], pq[onward], TN)
        pdv[rows] = dot(mix[onward, rows], pc[onward], TN)
    save(pdk, pdk_out)
    save(pdv, pdv_out)

    s_piece(1, 0)
    s_piece(1, 1)
    s_piece(1, 2)
    s_piece(1, 3)

    for rows, upto, onward in blocks:
        part[0, rows] = dot(mix[rows, upto], pv[upto], NN)
        part[1, rows] = dot(gmix[rows, upto], pk[upto], NN)
    loads[6].wait()
    loads[7].wait()
    mixings(rqs, rk, REPLY_HEADS, mix)
    rcs[...] = scale_rows(rw[...], reply_first, REPLY_HEADS)
    mixings(rcs, rv, REPLY_HEADS, gmix)
    for rows, upto, onward in blocks:
        rdv[rows] = dot(mix[onward, rows], rw[onward], TN).astype(BF16)
    save(rdv, rdv_out)
    for rows, upto, onward in blocks:
        rdk[rows] = dot(gmix[onward, rows], rq[onward], TN).astype(BF16)
    save(rdk, rdk_out)
    for rows, upto, onward in blocks:
        part[2, rows] = dot(mix[rows, upto], rv[upto], NN)
        part[3, rows] = dot(gmix[rows, upto], rk[upto], NN)

    collect(0, bef)
    before = bef[...].reshape(PROMPT_HEADS * E, E)
    po[...] = (part[0] + dot(by_head(pqs[...], PROMPT_HEADS), before, NN)).astype(BF16)
    save(po, po_out)
    wide = stack_wide(before, PROMPT_HEADS)
    pdq[...] = (part[1] + dot(by_head(pcs[...], PROMPT_HEADS), wide, NT)).astype(BF16)
    save(pdq, pdq_out)

    collect(1, aft)
    save(aft, aft_out)

    @pl.when(loops_back)
    def _():
        wait_bytes(fin.at[pl.ds(0, 15)], f_recv)

    @pl.when(jnp.logical_not(loops_back))
    def _():
        wait_bytes(fin, f_recv)

    final = fin[...].reshape(REPLY_HEADS * E, E).astype(BF16)
    out = part[2] + dot(by_head(rqs[...], REPLY_HEADS), final, NN)
    s = lax.broadcasted_iota(jnp.int32, (ROWS, E), 0)
    ro[...] = jnp.where((s // REPLY_HEADS) < length[0], out, 0.0).astype(BF16)
    save(ro, ro_out)
    wide = stack_wide(final, REPLY_HEADS)
    rdq[...] = (part[3] + dot(by_head(rcs[...], REPLY_HEADS), wide, NT)).astype(BF16)
    save(rdq, rdq_out)

    for k in range(2):
        wait_bytes(loc.at[k, pl.ds(0, NX - 1)], x_send.at[k])
        wait_bytes(yt.at[k, pl.ds(0, NY - 1)], y_send.at[k])
        wait_bytes(ys.at[k, pl.ds(0, NY - 1)], b_send.at[k])
        wait_bytes(xs.at[k, pl.ds(0, NX - 1)], s_send.at[k])
    wait_bytes(wl.at[pl.ds(0, NY - 1)], w_send)

    @pl.when(loops_back)
    def _():
        wait_bytes(fin.at[pl.ds(0, 15)], f_send)

    @pl.when(jnp.logical_not(loops_back))
    def _():
        wait_bytes(fin, f_send)

    @pl.when(gathers)
    def _():
        wait_bytes(wy.at[pl.ds(0, NZ - 1)], v_send)

        @pl.when(same_column)
        def _():
            wait_bytes(wt.at[0], u_send)

        @pl.when(jnp.logical_not(same_column))
        def _():
            wait_bytes(wt, u_send)

    @pl.when(jnp.logical_not(gathers))
    def _():
        wait_bytes(wy, v_send)

    for copy in saves:
        copy.wait()


def exchange(*args):
    whole = pl.BlockSpec(memory_space=pl.ANY)
    smem = pl.BlockSpec(memory_space=pltpu.SMEM)
    dma = pltpu.SemaphoreType.DMA
    heads = pltpu.VMEM((2, NX, NY, SL, E), F32)
    narrow = pltpu.VMEM((ROWS, E), BF16)
    wide = pltpu.VMEM((ROWS, E), F32)
    slices = pltpu.VMEM((2, NY, SL, E), F32)
    return pl.pallas_call(
        exchange_kernel,
        out_shape=tuple(
            [jax.ShapeDtypeStruct((ROWS, E), BF16)] * 6
            + [jax.ShapeDtypeStruct((ROWS, E), F32)] * 2
            + [jax.ShapeDtypeStruct((PROMPT_HEADS, NY, SL, E), BF16)]),
        in_specs=[whole] * 8 + [smem] * 2,
        out_specs=tuple([whole] * 9),
        scratch_shapes=[narrow] * 14 + [wide] * 2 + [
            pltpu.VMEM((PROMPT_HEADS, NY, SL, E), BF16),
            pltpu.VMEM((PROMPT_HEADS, NY, SL, E), BF16),
        ] + [narrow] * 5 + [
            pltpu.VMEM((ROWS, ROWS), BF16),
            pltpu.VMEM((ROWS, ROWS), BF16),
            pltpu.VMEM((4, ROWS, E), F32),
            pltpu.VMEM((NX, NY, SL, E), F32),
            heads, heads,
            slices, slices, slices, slices,
            heads, heads,
            pltpu.VMEM((SL, E), F32),
            pltpu.VMEM((16, SL, E), F32),
            pltpu.VMEM((NY, 2, SL, E), F32),
            pltpu.VMEM((NY, 2, SL, E), F32),
            pltpu.VMEM((16, 2, SL, E), F32),
            pltpu.VMEM((2, SL, E), F32),
            pltpu.VMEM((SL, E), F32),
            dma((8,)), dma((9,)),
            dma((2,)), dma((2, 4)), dma((2,)), dma((2,)),
            dma((2,)), dma((2, 4)), dma((2,)), dma((2,)),
            dma, dma, dma, dma, dma, dma, dma, dma,
        ],
        compiler_params=pltpu.CompilerParams(
            collective_id=0, has_side_effects=True),
        name="exchange",
    )(*args)


def finish_kernel(
    po_in, ro_in, pdq_in, rdq_in, rdk_in, rdv_in, pdk_in, pdv_in, aft_in, pk_in, pv_in,
    po_out, ro_out, pdq_out, rdq_out, rdk_out, rdv_out, pdk_out, pdv_out,
    po, ro, pdq, rdq, rdk, rdv, kpart, vpart, aft, pk, pv, pdk, pdv, in_sem, out_sem,
):
    ins = (aft_in, pv_in, pdk_in, pk_in, pdv_in, po_in, ro_in, pdq_in, rdq_in, rdk_in, rdv_in)
    held = (aft, pv, kpart, pk, vpart, po, ro, pdq, rdq, rdk, rdv)
    outs = (po_out, ro_out, pdq_out, rdq_out, rdk_out, rdv_out)
    loads = [pltpu.make_async_copy(src, dst, in_sem.at[n])
             for n, (src, dst) in enumerate(zip(ins, held))]
    for load in loads:
        load.start()
    saves = []

    def save(src, dst):
        copy = pltpu.make_async_copy(src, dst, out_sem.at[len(saves)])
        copy.start()
        saves.append(copy)

    loads[0].wait()
    loads[1].wait()
    wide = stack_wide(aft[...], PROMPT_HEADS)
    grad = dot(by_head(pv[...], PROMPT_HEADS), wide, NT)
    loads[2].wait()
    pdk[...] = (kpart[...] + grad).astype(BF16)
    save(pdk, pdk_out)
    loads[3].wait()
    grad = dot(by_head(pk[...], PROMPT_HEADS), aft[...], NN)
    loads[4].wait()
    pdv[...] = (vpart[...] + grad).astype(BF16)
    save(pdv, pdv_out)
    for n in range(6):
        loads[5 + n].wait()
        save(held[5 + n], outs[n])
    for copy in saves:
        copy.wait()


def finish(*args):
    whole = pl.BlockSpec(memory_space=pl.ANY)
    narrow = pltpu.VMEM((ROWS, E), BF16)
    wide = pltpu.VMEM((ROWS, E), F32)
    return pl.pallas_call(
        finish_kernel,
        out_shape=tuple([jax.ShapeDtypeStruct((ROWS, E), BF16)] * 8),
        in_specs=[whole] * 11,
        out_specs=tuple([whole] * 8),
        scratch_shapes=[narrow] * 6 + [wide] * 2 + [
            pltpu.VMEM((PROMPT_HEADS * E, E), BF16)] + [narrow] * 4 + [
            pltpu.SemaphoreType.DMA((11,)), pltpu.SemaphoreType.DMA((8,))],
        name="finish",
    )(*args)


def shards(
    prompt_query, prompt_key, prompt_value, prompt_cotangent,
    reply_query, reply_key, reply_value, reply_cotangent,
    reply_weight, reply_length,
):
    prompt_shape = prompt_query.shape
    reply_shape = reply_query.shape
    pq, pk, pv, pc, rq, rk, rv, rc = [
        a.reshape(ROWS, E)
        for a in (prompt_query, prompt_key, prompt_value, prompt_cotangent,
                  reply_query, reply_key, reply_value, reply_cotangent)
    ]
    parts = exchange(pq, pk, pv, pc, rq, rk, rv, rc, reply_weight, reply_length)
    after = parts[-1].reshape(PROMPT_HEADS * E, E)
    po, ro, pdq, rdq, rdk, rdv, pdk, pdv = finish(*parts[:-1], after, pk, pv)
    return (
        po.reshape(prompt_shape), ro.reshape(reply_shape),
        pdq.reshape(prompt_shape), pdk.reshape(prompt_shape), pdv.reshape(prompt_shape),
        rdq.reshape(reply_shape), rdk.reshape(reply_shape), rdv.reshape(reply_shape),
    )


def solution(mesh):
    prompt = P(("ctx", "head"), "resp", None)
    reply = P("resp", None, ("ctx", "head"), None)
    placed = (prompt,) * 4 + (reply,) * 4 + (P("resp"), P("resp"))
    return jax.shard_map(
        shards,
        mesh=mesh,
        in_specs=placed,
        out_specs=(prompt, reply, prompt, prompt, prompt, reply, reply, reply),
        check_vma=False,
    )
```

```python
import jax
import jax.numpy as jnp
from jax import lax
from jax.experimental import pallas as pl
from jax.experimental.pallas import tpu as pltpu
from jax.sharding import PartitionSpec as P

MESH = pl.DeviceIdType.MESH
F32 = jnp.float32
BF16 = jnp.bfloat16
NY, NX, NZ, NC = 8, 4, 8, 2
E = 128
ROWS = 1024
PROMPT_HEADS = 4
REPLY_HEADS = 2
BLK = 256
SL = E // NY
FAR = [4, 3, 5, 2, 6, 1, 7, 0]
NEAR = [0, 1, 7, 2, 6, 3, 5, 4]

NN = (((1,), (0,)), ((), ()))
NT = (((1,), (1,)), ((), ()))
TN = (((0,), (0,)), ((), ()))


def dot(a, b, dims):
    return lax.dot_general(a, b, dims, preferred_element_type=F32)


def scale_rows(x, first, heads):
    s = lax.broadcasted_iota(jnp.int32, x.shape, 0)
    pos = (first + s // heads).astype(F32)
    return (x.astype(F32) * lax.rsqrt(float(E) * (pos + 1.0))).astype(BF16)


def by_head(x, heads):
    period = lax.broadcasted_iota(jnp.int32, (16, E), 0) & (heads - 1)
    tiles = x.reshape(ROWS // 16, 16, E)
    parts = []
    for h in range(heads):
        keep = jnp.where(period == h, 1.0, 0.0).astype(BF16)
        parts.append((tiles * keep[None]).reshape(ROWS, E))
    return jnp.concatenate(parts, axis=1)


def reply_weighted(c, weight, length):
    s = lax.broadcasted_iota(jnp.int32, c.shape, 0)
    live = (s // REPLY_HEADS) < length
    return (weight * jnp.where(live, c.astype(F32), 0.0)).astype(BF16)


def wait_bytes(view, sem):
    pltpu.make_async_copy(view, view, sem).wait()


def pair_masks(heads):
    a = lax.broadcasted_iota(jnp.int32, (BLK, BLK), 0)
    b = lax.broadcasted_iota(jnp.int32, (BLK, BLK), 1)
    same = ((a ^ b) & (heads - 1)) == 0
    off = jnp.where(same, 1.0, 0.0)
    diag = jnp.where(a >= b, off, 0.0)
    return off.astype(BF16), diag.astype(BF16)


def mixings(left, right, heads, dest):
    off, diag = pair_masks(heads)
    for i in range(ROWS // BLK):
        rows = pl.ds(i * BLK, BLK)
        for j in range(i + 1):
            cols = pl.ds(j * BLK, BLK)
            part = dot(left[i * BLK:(i + 1) * BLK], right[j * BLK:(j + 1) * BLK], NT)
            dest[rows, cols] = part.astype(BF16) * (diag if i == j else off)


def stack_wide(state, heads):
    return jnp.concatenate([state[h * E:(h + 1) * E] for h in range(heads)], axis=1)


def exchange_kernel(
    pq_in, pk_in, pv_in, pc_in, rq_in, rk_in, rv_in, rc_in, weight, length,
    po_out, ro_out, pdq_out, rdq_out, rdk_out, rdv_out, pdk_out, pdv_out, aft_out,
    pq, pk, pv, pc, rq, rk, rv, rc,
    po, ro, pdq, rdq, rdk, rdv, pdk, pdv, aft, bef,
    pqs, pcs, rqs, rcs, rw, mix, gmix, part,
    raw, loc, xr, yt, yr, ys, yb, xs, st, zf, fin, wl, wp, ws, wy, wq, wt, wf,
    in_sem, out_sem,
    x_send, x_recv, y_send, y_recv, b_send, b_recv, s_send, s_recv,
    z_send, z_recv, f_send, f_recv, w_send, w_recv, v_send, v_recv, u_send, u_recv, c_send, c_recv,
):
    y = lax.axis_index("ctx")
    x = lax.axis_index("head")
    r = lax.axis_index("resp")
    z = r // 2
    c = r % 2
    fx = 2 * c + x // 2
    same_column = fx == x
    owner = (y, 2 * (x % 2) + c, 2 * z + x // 2)
    summer = (y, fx, 2 * z + x % 2)

    barrier = pltpu.get_barrier_semaphore()

    loads = [
        pltpu.make_async_copy(src, dst, in_sem.at[n])
        for n, (src, dst) in enumerate((
            (pk_in, pk), (pv_in, pv), (rq_in, rq), (rc_in, rc),
            (pq_in, pq), (pc_in, pc), (rk_in, rk), (rv_in, rv)))
    ]
    for load in loads:
        load.start()

    saves = []

    def save(src, dst):
        copy = pltpu.make_async_copy(src, dst, out_sem.at[len(saves)])
        copy.start()
        saves.append(copy)

    def send(src, dst, send_sem, recv_sem, device):
        pltpu.make_async_remote_copy(
            src_ref=src, dst_ref=dst, send_sem=send_sem, recv_sem=recv_sem,
            device_id=device, device_id_type=MESH).start()

    def signal(device):
        pl.semaphore_signal(barrier, inc=1, device_id=device, device_id_type=MESH)

    @pl.loop(1, NX)
    def _(d):
        signal((y, (x + d) % NX, r))

    @pl.loop(1, NY)
    def _(d):
        signal(((y + d) % NY, x, r))

    @pl.loop(1, NZ * NC)
    def _(d):
        signal((y, x, (r + d) % (NZ * NC)))

    @pl.when(jnp.logical_not(same_column))
    def _():
        signal(owner)
        signal(summer)

    block = y * NX + x
    prompt_first = block * (ROWS // PROMPT_HEADS)
    reply_first = NY * NX * (ROWS // PROMPT_HEADS)

    def states(k, left, right):
        wide = dot(left, by_head(right, PROMPT_HEADS), TN)
        for h in range(PROMPT_HEADS):
            raw[h] = wide[:, h * E:(h + 1) * E].reshape(NY, SL, E)
        for p in range(NY):
            row = (y + FAR[p]) % NY
            for h in range(PROMPT_HEADS):
                loc[k, h, p] = raw[h, row]

    def x_start(k):
        for piece in range(NY // 2):
            span = pl.ds(2 * piece, 2)

            @pl.loop(1, NX)
            def _(d):
                to = (x + d) % NX
                send(loc.at[k, to, span], xr.at[k, x, span],
                     x_send.at[k], x_recv.at[k, piece], (y, to, r))
        xr[k, x] = loc[k, x]

    def y_piece(k, piece):
        wait_bytes(xr.at[k, 0, pl.ds(0, 2 * (NX - 1))], x_recv.at[k, piece])
        for p in (2 * piece, 2 * piece + 1):
            yt[k, p] = (xr[k, 0, p] + xr[k, 1, p]) + (xr[k, 2, p] + xr[k, 3, p])
            if FAR[p]:
                send(yt.at[k, p], yr.at[k, y], y_send.at[k], y_recv.at[k],
                     ((y + FAR[p]) % NY, x, r))
            else:
                yr[k, y] = yt[k, p]

    def b_start(k):
        for rel in FAR[:-1]:
            to = (y + rel) % NY
            back = (NY - rel) % NY
            send(ys.at[k, to], yb.at[k, NEAR.index(back)],
                 b_send.at[k], b_recv.at[k, min(back, NY - back) - 1], (to, x, r))
        yb[k, 0] = ys[k, y]

    def s_piece(k, piece):
        first, count = ((0, 3), (3, 2), (5, 2), (7, 1))[piece]
        wait_bytes(yb.at[k, pl.ds(0, 1 if piece == 3 else 2)], b_recv.at[k, piece])
        for q in range(first, first + count):
            p = FAR.index(NEAR[q])
            running = yb[k, q]
            order = range(NX) if k == 0 else range(NX - 1, -1, -1)
            for n in order:
                xs[k, n, q] = running
                running = running + xr[k, n, p]
        span = pl.ds(first, count)

        @pl.loop(1, NX)
        def _(d):
            to = (x + d) % NX
            send(xs.at[k, to, span], st.at[k, x, span],
                 s_send.at[k], s_recv.at[k], (y, to, r))
        for q in range(first, first + count):
            st[k, x, q] = xs[k, x, q]

    def collect(k, dest):
        wait_bytes(st.at[k, pl.ds(0, NX - 1)], s_recv.at[k])
        for q in range(NY):
            row = (y + NEAR[q]) % NY
            for h in range(PROMPT_HEADS):
                dest[h, row] = st[k, h, q].astype(BF16)

    loads[0].wait()
    loads[1].wait()
    states(0, pk[...], pv[...])

    loads[2].wait()
    loads[3].wait()
    rw[...] = reply_weighted(rc[...], weight[0], length[0])
    rqs[...] = scale_rows(rq[...], reply_first, REPLY_HEADS)
    wide = dot(rqs[...], by_head(rw[...], REPLY_HEADS), TN)
    for i in range(REPLY_HEADS):
        wl[i] = wide[:, i * E:(i + 1) * E].reshape(NY, SL, E)

    near = NX - 1 + NY - 1 + NZ * NC - 1

    @pl.when(same_column)
    def _():
        pl.semaphore_wait(barrier, near)

    @pl.when(jnp.logical_not(same_column))
    def _():
        pl.semaphore_wait(barrier, near + 2)

    send(wl.at[1 - c], wp, c_send, c_recv, (y, x, 2 * z + 1 - c))
    x_start(0)

    loads[4].wait()
    loads[5].wait()
    pqs[...] = scale_rows(pq[...], prompt_first, PROMPT_HEADS)
    states(1, pqs[...], pc[...])
    x_start(1)

    wait_bytes(wp, c_recv)
    ws[...] = wl[c] + wp[...]
    for rel in FAR[:-1]:
        to = (y + rel) % NY
        send(ws.at[to], wy.at[y], w_send, w_recv, (to, x, r))
    wy[y] = ws[y]

    blocks = [(slice(i * BLK, (i + 1) * BLK), slice(0, (i + 1) * BLK), slice(i * BLK, ROWS))
              for i in range(ROWS // BLK)]

    mixings(pqs, pk, PROMPT_HEADS, mix)

    for piece in range(NY // 2):
        y_piece(0, piece)

    wait_bytes(wy.at[pl.ds(0, NY - 1)], w_recv)
    for rel in FAR[:-1]:
        to = (z + rel) % NZ
        send(wy.at[to], wq.at[z], v_send, v_recv, (y, x, 2 * to + c))
    wq[z] = wy[z]

    for piece in range(NY // 2):
        y_piece(1, piece)

    wait_bytes(yr.at[0, pl.ds(0, NY - 1)], y_recv.at[0])
    running = jnp.zeros((SL, E), F32)
    for n in range(NY):
        ys[0, n] = running
        running = running + yr[0, n]
    zf[z] = running
    b_start(0)

    @pl.loop(1, NZ)
    def _(d):
        send(zf.at[z], zf.at[z], z_send, z_recv, (y, x, 2 * ((z + d) % NZ) + c))

    pcs[...] = scale_rows(pc[...], prompt_first, PROMPT_HEADS)
    mixings(pcs, pv, PROMPT_HEADS, gmix)
    for rows, upto, onward in blocks:
        part[0, rows] = dot(mix[rows, upto], pv[upto], NN)
        part[1, rows] = dot(gmix[rows, upto], pk[upto], NN)

    s_piece(0, 0)
    wait_bytes(wq.at[pl.ds(0, NZ - 1)], v_recv)
    total = wq[0]
    for n in range(1, NZ):
        total = total + wq[n]
    wt[...] = total

    @pl.when(jnp.logical_not(same_column))
    def _():
        send(wt, wf, u_send, u_recv, owner)

    @pl.when(same_column)
    def _():
        wf[...] = wt[...]

    s_piece(0, 1)
    s_piece(0, 2)
    s_piece(0, 3)

    for rows, upto, onward in blocks:
        pdk[rows] = dot(gmix[onward, rows], pq[onward], TN)
        pdv[rows] = dot(mix[onward, rows], pc[onward], TN)
    save(pdk, pdk_out)
    save(pdv, pdv_out)

    wait_bytes(yr.at[1, pl.ds(0, NY - 1)], y_recv.at[1])

    @pl.when(jnp.logical_not(same_column))
    def _():
        wait_bytes(wf, u_recv)

    running = wf[...]
    for n in reversed(range(NY)):
        ys[1, n] = running
        running = running + yr[1, n]
    b_start(1)

    wait_bytes(zf.at[pl.ds(0, NZ - 1)], z_recv)
    for rel in FAR:
        row = (y + rel) % NY
        for core in range(NC):
            def go():
                send(zf.at[row], fin.at[(x % 2) * NY + y], f_send, f_recv,
                     (row, fx, 2 * z + core))
            if rel:
                go()
            else:
                pl.when(jnp.logical_not(same_column & (c == core)))(go)

    @pl.when(same_column)
    def _():
        fin[(x % 2) * NY + y] = zf[y]

    loads[6].wait()
    loads[7].wait()
    mixings(rqs, rk, REPLY_HEADS, mix)

    s_piece(1, 0)
    s_piece(1, 1)
    s_piece(1, 2)
    s_piece(1, 3)

    rcs[...] = scale_rows(rw[...], reply_first, REPLY_HEADS)
    mixings(rcs, rv, REPLY_HEADS, gmix)
    for rows, upto, onward in blocks:
        rdv[rows] = dot(mix[onward, rows], rw[onward], TN).astype(BF16)
    save(rdv, rdv_out)
    for rows, upto, onward in blocks:
        rdk[rows] = dot(gmix[onward, rows], rq[onward], TN).astype(BF16)
    save(rdk, rdk_out)
    for rows, upto, onward in blocks:
        part[2, rows] = dot(mix[rows, upto], rv[upto], NN)
        part[3, rows] = dot(gmix[rows, upto], rk[upto], NN)

    collect(0, bef)
    before = bef[...].reshape(PROMPT_HEADS * E, E)
    po[...] = (part[0] + dot(by_head(pqs[...], PROMPT_HEADS), before, NN)).astype(BF16)
    save(po, po_out)
    wide = stack_wide(before, PROMPT_HEADS)
    pdq[...] = (part[1] + dot(by_head(pcs[...], PROMPT_HEADS), wide, NT)).astype(BF16)
    save(pdq, pdq_out)

    collect(1, aft)
    save(aft, aft_out)

    @pl.when(same_column)
    def _():
        wait_bytes(fin.at[pl.ds(0, 15)], f_recv)

    @pl.when(jnp.logical_not(same_column))
    def _():
        wait_bytes(fin, f_recv)

    final = fin[...].reshape(REPLY_HEADS * E, E).astype(BF16)
    out = part[2] + dot(by_head(rqs[...], REPLY_HEADS), final, NN)
    s = lax.broadcasted_iota(jnp.int32, (ROWS, E), 0)
    ro[...] = jnp.where((s // REPLY_HEADS) < length[0], out, 0.0).astype(BF16)
    save(ro, ro_out)
    wide = stack_wide(final, REPLY_HEADS)
    rdq[...] = (part[3] + dot(by_head(rcs[...], REPLY_HEADS), wide, NT)).astype(BF16)
    save(rdq, rdq_out)

    for k in range(2):
        wait_bytes(loc.at[k, pl.ds(0, NX - 1)], x_send.at[k])
        wait_bytes(yt.at[k, pl.ds(0, NY - 1)], y_send.at[k])
        wait_bytes(ys.at[k, pl.ds(0, NY - 1)], b_send.at[k])
        wait_bytes(xs.at[k, pl.ds(0, NX - 1)], s_send.at[k])
    wait_bytes(wp, c_send)
    wait_bytes(wy.at[pl.ds(0, NY - 1)], w_send)
    wait_bytes(wq.at[pl.ds(0, NZ - 1)], v_send)
    wait_bytes(zf.at[pl.ds(0, NZ - 1)], z_send)

    @pl.when(same_column)
    def _():
        wait_bytes(fin.at[pl.ds(0, 15)], f_send)

    @pl.when(jnp.logical_not(same_column))
    def _():
        wait_bytes(fin, f_send)
        wait_bytes(wt, u_send)

    for copy in saves:
        copy.wait()


def exchange(*args):
    whole = pl.BlockSpec(memory_space=pl.ANY)
    smem = pl.BlockSpec(memory_space=pltpu.SMEM)
    dma = pltpu.SemaphoreType.DMA
    heads = pltpu.VMEM((2, NX, NY, SL, E), F32)
    narrow = pltpu.VMEM((ROWS, E), BF16)
    wide = pltpu.VMEM((ROWS, E), F32)
    slices = pltpu.VMEM((2, NY, SL, E), F32)
    return pl.pallas_call(
        exchange_kernel,
        out_shape=tuple(
            [jax.ShapeDtypeStruct((ROWS, E), BF16)] * 6
            + [jax.ShapeDtypeStruct((ROWS, E), F32)] * 2
            + [jax.ShapeDtypeStruct((PROMPT_HEADS, NY, SL, E), BF16)]),
        in_specs=[whole] * 8 + [smem] * 2,
        out_specs=tuple([whole] * 9),
        scratch_shapes=[narrow] * 14 + [wide] * 2 + [
            pltpu.VMEM((PROMPT_HEADS, NY, SL, E), BF16),
            pltpu.VMEM((PROMPT_HEADS, NY, SL, E), BF16),
        ] + [narrow] * 5 + [
            pltpu.VMEM((ROWS, ROWS), BF16),
            pltpu.VMEM((ROWS, ROWS), BF16),
            pltpu.VMEM((4, ROWS, E), F32),
            pltpu.VMEM((NX, NY, SL, E), F32),
            heads, heads,
            slices, slices, slices, slices,
            heads, heads,
            pltpu.VMEM((NZ, SL, E), F32),
            pltpu.VMEM((16, SL, E), F32),
            slices,
            pltpu.VMEM((NY, SL, E), F32),
            pltpu.VMEM((NY, SL, E), F32),
            pltpu.VMEM((NY, SL, E), F32),
            pltpu.VMEM((NZ, SL, E), F32),
            pltpu.VMEM((SL, E), F32),
            pltpu.VMEM((SL, E), F32),
            dma((8,)), dma((9,)),
            dma((2,)), dma((2, 4)), dma((2,)), dma((2,)),
            dma((2,)), dma((2, 4)), dma((2,)), dma((2,)),
            dma, dma, dma, dma, dma, dma, dma, dma, dma, dma, dma, dma,
        ],
        compiler_params=pltpu.CompilerParams(
            collective_id=0, has_side_effects=True),
        name="exchange",
    )(*args)


def finish_kernel(
    po_in, ro_in, pdq_in, rdq_in, rdk_in, rdv_in, pdk_in, pdv_in, aft_in, pk_in, pv_in,
    po_out, ro_out, pdq_out, rdq_out, rdk_out, rdv_out, pdk_out, pdv_out,
    po, ro, pdq, rdq, rdk, rdv, kpart, vpart, aft, pk, pv, pdk, pdv, in_sem, out_sem,
):
    ins = (aft_in, pv_in, pdk_in, pk_in, pdv_in, po_in, ro_in, pdq_in, rdq_in, rdk_in, rdv_in)
    held = (aft, pv, kpart, pk, vpart, po, ro, pdq, rdq, rdk, rdv)
    outs = (po_out, ro_out, pdq_out, rdq_out, rdk_out, rdv_out)
    loads = [pltpu.make_async_copy(src, dst, in_sem.at[n])
             for n, (src, dst) in enumerate(zip(ins, held))]
    for load in loads:
        load.start()
    saves = []

    def save(src, dst):
        copy = pltpu.make_async_copy(src, dst, out_sem.at[len(saves)])
        copy.start()
        saves.append(copy)

    loads[0].wait()
    loads[1].wait()
    wide = stack_wide(aft[...], PROMPT_HEADS)
    grad = dot(by_head(pv[...], PROMPT_HEADS), wide, NT)
    loads[2].wait()
    pdk[...] = (kpart[...] + grad).astype(BF16)
    save(pdk, pdk_out)
    loads[3].wait()
    grad = dot(by_head(pk[...], PROMPT_HEADS), aft[...], NN)
    loads[4].wait()
    pdv[...] = (vpart[...] + grad).astype(BF16)
    save(pdv, pdv_out)
    for n in range(6):
        loads[5 + n].wait()
        save(held[5 + n], outs[n])
    for copy in saves:
        copy.wait()


def finish(*args):
    whole = pl.BlockSpec(memory_space=pl.ANY)
    narrow = pltpu.VMEM((ROWS, E), BF16)
    wide = pltpu.VMEM((ROWS, E), F32)
    return pl.pallas_call(
        finish_kernel,
        out_shape=tuple([jax.ShapeDtypeStruct((ROWS, E), BF16)] * 8),
        in_specs=[whole] * 11,
        out_specs=tuple([whole] * 8),
        scratch_shapes=[narrow] * 6 + [wide] * 2 + [
            pltpu.VMEM((PROMPT_HEADS * E, E), BF16)] + [narrow] * 4 + [
            pltpu.SemaphoreType.DMA((11,)), pltpu.SemaphoreType.DMA((8,))],
        name="finish",
    )(*args)


def shards(
    prompt_query, prompt_key, prompt_value, prompt_cotangent,
    reply_query, reply_key, reply_value, reply_cotangent,
    reply_weight, reply_length,
):
    prompt_shape = prompt_query.shape
    reply_shape = reply_query.shape
    pq, pk, pv, pc, rq, rk, rv, rc = [
        a.reshape(ROWS, E)
        for a in (prompt_query, prompt_key, prompt_value, prompt_cotangent,
                  reply_query, reply_key, reply_value, reply_cotangent)
    ]
    parts = exchange(pq, pk, pv, pc, rq, rk, rv, rc, reply_weight, reply_length)
    after = parts[-1].reshape(PROMPT_HEADS * E, E)
    po, ro, pdq, rdq, rdk, rdv, pdk, pdv = finish(*parts[:-1], after, pk, pv)
    return (
        po.reshape(prompt_shape), ro.reshape(reply_shape),
        pdq.reshape(prompt_shape), pdk.reshape(prompt_shape), pdv.reshape(prompt_shape),
        rdq.reshape(reply_shape), rdk.reshape(reply_shape), rdv.reshape(reply_shape),
    )


def solution(mesh):
    prompt = P(("ctx", "head"), "resp", None)
    reply = P("resp", None, ("ctx", "head"), None)
    placed = (prompt,) * 4 + (reply,) * 4 + (P("resp"), P("resp"))
    return jax.shard_map(
        shards,
        mesh=mesh,
        in_specs=placed,
        out_specs=(prompt, reply, prompt, prompt, prompt, reply, reply, reply),
        check_vma=False,
    )
```

```python
import jax
import jax.numpy as jnp
from jax import lax
from jax.experimental import pallas as pl
from jax.experimental.pallas import tpu as pltpu
from jax.sharding import PartitionSpec as P

MESH = pl.DeviceIdType.MESH
F32 = jnp.float32
BF16 = jnp.bfloat16
NY, NX, NZ, NC = 8, 4, 8, 2
E = 128
ROWS = 1024
PROMPT_HEADS = 4
REPLY_HEADS = 2
BLK = 256
SL = E // NY
FAR = [4, 3, 5, 2, 6, 1, 7, 0]
NEAR = [0, 1, 7, 2, 6, 3, 5, 4]

NN = (((1,), (0,)), ((), ()))
NT = (((1,), (1,)), ((), ()))
TN = (((0,), (0,)), ((), ()))


def dot(a, b, dims):
    return lax.dot_general(a, b, dims, preferred_element_type=F32)


def scale_rows(x, first, heads):
    s = lax.broadcasted_iota(jnp.int32, x.shape, 0)
    pos = (first + s // heads).astype(F32)
    return (x.astype(F32) * lax.rsqrt(float(E) * (pos + 1.0))).astype(BF16)


def by_head(x, heads):
    period = lax.broadcasted_iota(jnp.int32, (16, E), 0) & (heads - 1)
    tiles = x.reshape(ROWS // 16, 16, E)
    parts = []
    for h in range(heads):
        keep = jnp.where(period == h, 1.0, 0.0).astype(BF16)
        parts.append((tiles * keep[None]).reshape(ROWS, E))
    return jnp.concatenate(parts, axis=1)


def reply_weighted(c, weight, length):
    s = lax.broadcasted_iota(jnp.int32, c.shape, 0)
    live = (s // REPLY_HEADS) < length
    return (weight * jnp.where(live, c.astype(F32), 0.0)).astype(BF16)


def wait_bytes(view, sem):
    pltpu.make_async_copy(view, view, sem).wait()


def pair_masks(heads):
    a = lax.broadcasted_iota(jnp.int32, (BLK, BLK), 0)
    b = lax.broadcasted_iota(jnp.int32, (BLK, BLK), 1)
    same = ((a ^ b) & (heads - 1)) == 0
    off = jnp.where(same, 1.0, 0.0)
    diag = jnp.where(a >= b, off, 0.0)
    return off.astype(BF16), diag.astype(BF16)


def mixings(left, right, heads, dest):
    off, diag = pair_masks(heads)
    for i in range(ROWS // BLK):
        rows = pl.ds(i * BLK, BLK)
        for j in range(i + 1):
            cols = pl.ds(j * BLK, BLK)
            part = dot(left[i * BLK:(i + 1) * BLK], right[j * BLK:(j + 1) * BLK], NT)
            dest[rows, cols] = part.astype(BF16) * (diag if i == j else off)


def stack_wide(state, heads):
    return jnp.concatenate([state[h * E:(h + 1) * E] for h in range(heads)], axis=1)


def exchange_kernel(
    pq_in, pk_in, pv_in, pc_in, rq_in, rk_in, rv_in, rc_in, weight, length,
    po_out, ro_out, pdq_out, rdq_out, rdk_out, rdv_out, pdk_out, pdv_out, aft_out,
    pq, pk, pv, pc, rq, rk, rv, rc,
    po, ro, pdq, rdq, rdk, rdv, pdk, pdv, aft, bef,
    pqs, pcs, rqs, rcs, rw, mix, gmix, part,
    raw, loc, xr, yt, yr, ys, yb, xs, st, zf, fin, wl, wp, ws, wy, wq, wt, wf,
    in_sem, out_sem,
    x_send, x_recv, y_send, y_recv, b_send, b_recv, s_send, s_recv,
    z_send, z_recv, f_send, f_recv, w_send, w_recv, v_send, v_recv, u_send, u_recv, c_send, c_recv,
):
    y = lax.axis_index("ctx")
    x = lax.axis_index("head")
    r = lax.axis_index("resp")
    z = r // 2
    c = r % 2
    fx = 2 * c + x // 2
    same_column = fx == x
    owner = (y, 2 * (x % 2) + c, 2 * z + x // 2)
    summer = (y, fx, 2 * z + x % 2)

    barrier = pltpu.get_barrier_semaphore()

    loads = [
        pltpu.make_async_copy(src, dst, in_sem.at[n])
        for n, (src, dst) in enumerate((
            (pk_in, pk), (pv_in, pv), (rq_in, rq), (rc_in, rc),
            (pq_in, pq), (pc_in, pc), (rk_in, rk), (rv_in, rv)))
    ]
    for load in loads:
        load.start()

    saves = []

    def save(src, dst):
        copy = pltpu.make_async_copy(src, dst, out_sem.at[len(saves)])
        copy.start()
        saves.append(copy)

    def send(src, dst, send_sem, recv_sem, device):
        pltpu.make_async_remote_copy(
            src_ref=src, dst_ref=dst, send_sem=send_sem, recv_sem=recv_sem,
            device_id=device, device_id_type=MESH).start()

    def signal(device):
        pl.semaphore_signal(barrier, inc=1, device_id=device, device_id_type=MESH)

    @pl.loop(1, NX)
    def _(d):
        signal((y, (x + d) % NX, r))

    @pl.loop(1, NY)
    def _(d):
        signal(((y + d) % NY, x, r))

    @pl.loop(1, NZ * NC)
    def _(d):
        signal((y, x, (r + d) % (NZ * NC)))

    @pl.when(jnp.logical_not(same_column))
    def _():
        signal(owner)
        signal(summer)

    block = y * NX + x
    prompt_first = block * (ROWS // PROMPT_HEADS)
    reply_first = NY * NX * (ROWS // PROMPT_HEADS)

    def states(k, left, right):
        wide = dot(left, by_head(right, PROMPT_HEADS), TN)
        for h in range(PROMPT_HEADS):
            raw[h] = wide[:, h * E:(h + 1) * E].reshape(NY, SL, E)
        for p in range(NY):
            row = (y + FAR[p]) % NY
            for h in range(PROMPT_HEADS):
                loc[k, h, p] = raw[h, row]

    def x_start(k):
        for piece in range(NY // 2):
            span = pl.ds(2 * piece, 2)

            @pl.loop(1, NX)
            def _(d):
                to = (x + d) % NX
                send(loc.at[k, to, span], xr.at[k, x, span],
                     x_send.at[k], x_recv.at[k, piece], (y, to, r))
        xr[k, x] = loc[k, x]

    def y_piece(k, piece):
        wait_bytes(xr.at[k, 0, pl.ds(0, 2 * (NX - 1))], x_recv.at[k, piece])
        for p in (2 * piece, 2 * piece + 1):
            yt[k, p] = (xr[k, 0, p] + xr[k, 1, p]) + (xr[k, 2, p] + xr[k, 3, p])
            if FAR[p]:
                send(yt.at[k, p], yr.at[k, y], y_send.at[k], y_recv.at[k],
                     ((y + FAR[p]) % NY, x, r))
            else:
                yr[k, y] = yt[k, p]

    def b_start(k):
        for rel in FAR[:-1]:
            to = (y + rel) % NY
            back = (NY - rel) % NY
            send(ys.at[k, to], yb.at[k, NEAR.index(back)],
                 b_send.at[k], b_recv.at[k, min(back, NY - back) - 1], (to, x, r))
        yb[k, 0] = ys[k, y]

    def s_piece(k, piece):
        first, count = ((0, 3), (3, 2), (5, 2), (7, 1))[piece]
        wait_bytes(yb.at[k, pl.ds(0, 1 if piece == 3 else 2)], b_recv.at[k, piece])
        for q in range(first, first + count):
            p = FAR.index(NEAR[q])
            running = yb[k, q]
            order = range(NX) if k == 0 else range(NX - 1, -1, -1)
            for n in order:
                xs[k, n, q] = running
                running = running + xr[k, n, p]
        span = pl.ds(first, count)

        @pl.loop(1, NX)
        def _(d):
            to = (x + d) % NX
            send(xs.at[k, to, span], st.at[k, x, span],
                 s_send.at[k], s_recv.at[k], (y, to, r))
        for q in range(first, first + count):
            st[k, x, q] = xs[k, x, q]

    def collect(k, dest):
        wait_bytes(st.at[k, pl.ds(0, NX - 1)], s_recv.at[k])
        for q in range(NY):
            row = (y + NEAR[q]) % NY
            for h in range(PROMPT_HEADS):
                dest[h, row] = st[k, h, q].astype(BF16)

    loads[0].wait()
    loads[1].wait()
    states(0, pk[...], pv[...])

    loads[2].wait()
    loads[3].wait()
    rw[...] = reply_weighted(rc[...], weight[0], length[0])
    rqs[...] = scale_rows(rq[...], reply_first, REPLY_HEADS)
    wide = dot(rqs[...], by_head(rw[...], REPLY_HEADS), TN)
    for i in range(REPLY_HEADS):
        wl[i] = wide[:, i * E:(i + 1) * E].reshape(NY, SL, E)

    near = NX - 1 + NY - 1 + NZ * NC - 1

    @pl.when(same_column)
    def _():
        pl.semaphore_wait(barrier, near)

    @pl.when(jnp.logical_not(same_column))
    def _():
        pl.semaphore_wait(barrier, near + 2)

    send(wl.at[1 - c], wp, c_send, c_recv, (y, x, 2 * z + 1 - c))
    x_start(0)

    loads[4].wait()
    loads[5].wait()
    pqs[...] = scale_rows(pq[...], prompt_first, PROMPT_HEADS)
    states(1, pqs[...], pc[...])
    x_start(1)

    wait_bytes(wp, c_recv)
    ws[...] = wl[c] + wp[...]
    for rel in FAR[:-1]:
        to = (y + rel) % NY
        send(ws.at[to], wy.at[y], w_send, w_recv, (to, x, r))
    wy[y] = ws[y]

    blocks = [(slice(i * BLK, (i + 1) * BLK), slice(0, (i + 1) * BLK), slice(i * BLK, ROWS))
              for i in range(ROWS // BLK)]

    mixings(pqs, pk, PROMPT_HEADS, mix)

    for piece in range(3):
        y_piece(0, piece)

    wait_bytes(wy.at[pl.ds(0, NY - 1)], w_recv)
    for rel in FAR[:-1]:
        to = (z + rel) % NZ
        send(wy.at[to], wq.at[z], v_send, v_recv, (y, x, 2 * to + c))
    wq[z] = wy[z]

    y_piece(0, 3)
    for piece in range(NY // 2):
        y_piece(1, piece)

    wait_bytes(yr.at[0, pl.ds(0, NY - 1)], y_recv.at[0])
    running = jnp.zeros((SL, E), F32)
    for n in range(NY):
        ys[0, n] = running
        running = running + yr[0, n]
    zf[z] = running
    b_start(0)

    @pl.loop(1, NZ)
    def _(d):
        send(zf.at[z], zf.at[z], z_send, z_recv, (y, x, 2 * ((z + d) % NZ) + c))

    pcs[...] = scale_rows(pc[...], prompt_first, PROMPT_HEADS)
    mixings(pcs, pv, PROMPT_HEADS, gmix)

    wait_bytes(wq.at[pl.ds(0, NZ - 1)], v_recv)
    total = wq[0]
    for n in range(1, NZ):
        total = total + wq[n]
    wt[...] = total

    @pl.when(jnp.logical_not(same_column))
    def _():
        send(wt, wf, u_send, u_recv, owner)

    @pl.when(same_column)
    def _():
        wf[...] = wt[...]

    for rows, upto, onward in blocks:
        part[0, rows] = dot(mix[rows, upto], pv[upto], NN)
        part[1, rows] = dot(gmix[rows, upto], pk[upto], NN)

    s_piece(0, 0)
    s_piece(0, 1)
    s_piece(0, 2)
    s_piece(0, 3)

    wait_bytes(yr.at[1, pl.ds(0, NY - 1)], y_recv.at[1])

    @pl.when(jnp.logical_not(same_column))
    def _():
        wait_bytes(wf, u_recv)

    running = wf[...]
    for n in reversed(range(NY)):
        ys[1, n] = running
        running = running + yr[1, n]
    b_start(1)

    wait_bytes(zf.at[pl.ds(0, NZ - 1)], z_recv)
    for rel in FAR:
        row = (y + rel) % NY
        for core in range(NC):
            def go():
                send(zf.at[row], fin.at[(x % 2) * NY + y], f_send, f_recv,
                     (row, fx, 2 * z + core))
            if rel:
                go()
            else:
                pl.when(jnp.logical_not(same_column & (c == core)))(go)

    @pl.when(same_column)
    def _():
        fin[(x % 2) * NY + y] = zf[y]

    for rows, upto, onward in blocks:
        pdk[rows] = dot(gmix[onward, rows], pq[onward], TN)
        pdv[rows] = dot(mix[onward, rows], pc[onward], TN)
    save(pdk, pdk_out)
    save(pdv, pdv_out)

    loads[6].wait()
    loads[7].wait()
    mixings(rqs, rk, REPLY_HEADS, mix)

    s_piece(1, 0)
    s_piece(1, 1)
    s_piece(1, 2)
    s_piece(1, 3)

    rcs[...] = scale_rows(rw[...], reply_first, REPLY_HEADS)
    mixings(rcs, rv, REPLY_HEADS, gmix)
    for rows, upto, onward in blocks:
        rdv[rows] = dot(mix[onward, rows], rw[onward], TN).astype(BF16)
    save(rdv, rdv_out)
    for rows, upto, onward in blocks:
        rdk[rows] = dot(gmix[onward, rows], rq[onward], TN).astype(BF16)
    save(rdk, rdk_out)
    for rows, upto, onward in blocks:
        part[2, rows] = dot(mix[rows, upto], rv[upto], NN)
        part[3, rows] = dot(gmix[rows, upto], rk[upto], NN)

    collect(0, bef)
    before = bef[...].reshape(PROMPT_HEADS * E, E)
    po[...] = (part[0] + dot(by_head(pqs[...], PROMPT_HEADS), before, NN)).astype(BF16)
    save(po, po_out)
    wide = stack_wide(before, PROMPT_HEADS)
    pdq[...] = (part[1] + dot(by_head(pcs[...], PROMPT_HEADS), wide, NT)).astype(BF16)
    save(pdq, pdq_out)

    collect(1, aft)
    save(aft, aft_out)

    @pl.when(same_column)
    def _():
        wait_bytes(fin.at[pl.ds(0, 15)], f_recv)

    @pl.when(jnp.logical_not(same_column))
    def _():
        wait_bytes(fin, f_recv)

    final = fin[...].reshape(REPLY_HEADS * E, E).astype(BF16)
    out = part[2] + dot(by_head(rqs[...], REPLY_HEADS), final, NN)
    s = lax.broadcasted_iota(jnp.int32, (ROWS, E), 0)
    ro[...] = jnp.where((s // REPLY_HEADS) < length[0], out, 0.0).astype(BF16)
    save(ro, ro_out)
    wide = stack_wide(final, REPLY_HEADS)
    rdq[...] = (part[3] + dot(by_head(rcs[...], REPLY_HEADS), wide, NT)).astype(BF16)
    save(rdq, rdq_out)

    for k in range(2):
        wait_bytes(loc.at[k, pl.ds(0, NX - 1)], x_send.at[k])
        wait_bytes(yt.at[k, pl.ds(0, NY - 1)], y_send.at[k])
        wait_bytes(ys.at[k, pl.ds(0, NY - 1)], b_send.at[k])
        wait_bytes(xs.at[k, pl.ds(0, NX - 1)], s_send.at[k])
    wait_bytes(wp, c_send)
    wait_bytes(wy.at[pl.ds(0, NY - 1)], w_send)
    wait_bytes(wq.at[pl.ds(0, NZ - 1)], v_send)
    wait_bytes(zf.at[pl.ds(0, NZ - 1)], z_send)

    @pl.when(same_column)
    def _():
        wait_bytes(fin.at[pl.ds(0, 15)], f_send)

    @pl.when(jnp.logical_not(same_column))
    def _():
        wait_bytes(fin, f_send)
        wait_bytes(wt, u_send)

    for copy in saves:
        copy.wait()


def exchange(*args):
    whole = pl.BlockSpec(memory_space=pl.ANY)
    smem = pl.BlockSpec(memory_space=pltpu.SMEM)
    dma = pltpu.SemaphoreType.DMA
    heads = pltpu.VMEM((2, NX, NY, SL, E), F32)
    narrow = pltpu.VMEM((ROWS, E), BF16)
    wide = pltpu.VMEM((ROWS, E), F32)
    slices = pltpu.VMEM((2, NY, SL, E), F32)
    return pl.pallas_call(
        exchange_kernel,
        out_shape=tuple(
            [jax.ShapeDtypeStruct((ROWS, E), BF16)] * 6
            + [jax.ShapeDtypeStruct((ROWS, E), F32)] * 2
            + [jax.ShapeDtypeStruct((PROMPT_HEADS, NY, SL, E), BF16)]),
        in_specs=[whole] * 8 + [smem] * 2,
        out_specs=tuple([whole] * 9),
        scratch_shapes=[narrow] * 14 + [wide] * 2 + [
            pltpu.VMEM((PROMPT_HEADS, NY, SL, E), BF16),
            pltpu.VMEM((PROMPT_HEADS, NY, SL, E), BF16),
        ] + [narrow] * 5 + [
            pltpu.VMEM((ROWS, ROWS), BF16),
            pltpu.VMEM((ROWS, ROWS), BF16),
            pltpu.VMEM((4, ROWS, E), F32),
            pltpu.VMEM((NX, NY, SL, E), F32),
            heads, heads,
            slices, slices, slices, slices,
            heads, heads,
            pltpu.VMEM((NZ, SL, E), F32),
            pltpu.VMEM((16, SL, E), F32),
            slices,
            pltpu.VMEM((NY, SL, E), F32),
            pltpu.VMEM((NY, SL, E), F32),
            pltpu.VMEM((NY, SL, E), F32),
            pltpu.VMEM((NZ, SL, E), F32),
            pltpu.VMEM((SL, E), F32),
            pltpu.VMEM((SL, E), F32),
            dma((8,)), dma((9,)),
            dma((2,)), dma((2, 4)), dma((2,)), dma((2,)),
            dma((2,)), dma((2, 4)), dma((2,)), dma((2,)),
            dma, dma, dma, dma, dma, dma, dma, dma, dma, dma, dma, dma,
        ],
        compiler_params=pltpu.CompilerParams(
            collective_id=0, has_side_effects=True),
        name="exchange",
    )(*args)


def finish_kernel(
    po_in, ro_in, pdq_in, rdq_in, rdk_in, rdv_in, pdk_in, pdv_in, aft_in, pk_in, pv_in,
    po_out, ro_out, pdq_out, rdq_out, rdk_out, rdv_out, pdk_out, pdv_out,
    po, ro, pdq, rdq, rdk, rdv, kpart, vpart, aft, pk, pv, pdk, pdv, in_sem, out_sem,
):
    ins = (aft_in, pv_in, pdk_in, pk_in, pdv_in, po_in, ro_in, pdq_in, rdq_in, rdk_in, rdv_in)
    held = (aft, pv, kpart, pk, vpart, po, ro, pdq, rdq, rdk, rdv)
    outs = (po_out, ro_out, pdq_out, rdq_out, rdk_out, rdv_out)
    loads = [pltpu.make_async_copy(src, dst, in_sem.at[n])
             for n, (src, dst) in enumerate(zip(ins, held))]
    for load in loads:
        load.start()
    saves = []

    def save(src, dst):
        copy = pltpu.make_async_copy(src, dst, out_sem.at[len(saves)])
        copy.start()
        saves.append(copy)

    loads[0].wait()
    loads[1].wait()
    wide = stack_wide(aft[...], PROMPT_HEADS)
    grad = dot(by_head(pv[...], PROMPT_HEADS), wide, NT)
    loads[2].wait()
    pdk[...] = (kpart[...] + grad).astype(BF16)
    save(pdk, pdk_out)
    loads[3].wait()
    grad = dot(by_head(pk[...], PROMPT_HEADS), aft[...], NN)
    loads[4].wait()
    pdv[...] = (vpart[...] + grad).astype(BF16)
    save(pdv, pdv_out)
    for n in range(6):
        loads[5 + n].wait()
        save(held[5 + n], outs[n])
    for copy in saves:
        copy.wait()


def finish(*args):
    whole = pl.BlockSpec(memory_space=pl.ANY)
    narrow = pltpu.VMEM((ROWS, E), BF16)
    wide = pltpu.VMEM((ROWS, E), F32)
    return pl.pallas_call(
        finish_kernel,
        out_shape=tuple([jax.ShapeDtypeStruct((ROWS, E), BF16)] * 8),
        in_specs=[whole] * 11,
        out_specs=tuple([whole] * 8),
        scratch_shapes=[narrow] * 6 + [wide] * 2 + [
            pltpu.VMEM((PROMPT_HEADS * E, E), BF16)] + [narrow] * 4 + [
            pltpu.SemaphoreType.DMA((11,)), pltpu.SemaphoreType.DMA((8,))],
        name="finish",
    )(*args)


def shards(
    prompt_query, prompt_key, prompt_value, prompt_cotangent,
    reply_query, reply_key, reply_value, reply_cotangent,
    reply_weight, reply_length,
):
    prompt_shape = prompt_query.shape
    reply_shape = reply_query.shape
    pq, pk, pv, pc, rq, rk, rv, rc = [
        a.reshape(ROWS, E)
        for a in (prompt_query, prompt_key, prompt_value, prompt_cotangent,
                  reply_query, reply_key, reply_value, reply_cotangent)
    ]
    parts = exchange(pq, pk, pv, pc, rq, rk, rv, rc, reply_weight, reply_length)
    after = parts[-1].reshape(PROMPT_HEADS * E, E)
    po, ro, pdq, rdq, rdk, rdv, pdk, pdv = finish(*parts[:-1], after, pk, pv)
    return (
        po.reshape(prompt_shape), ro.reshape(reply_shape),
        pdq.reshape(prompt_shape), pdk.reshape(prompt_shape), pdv.reshape(prompt_shape),
        rdq.reshape(reply_shape), rdk.reshape(reply_shape), rdv.reshape(reply_shape),
    )


def solution(mesh):
    prompt = P(("ctx", "head"), "resp", None)
    reply = P("resp", None, ("ctx", "head"), None)
    placed = (prompt,) * 4 + (reply,) * 4 + (P("resp"), P("resp"))
    return jax.shard_map(
        shards,
        mesh=mesh,
        in_specs=placed,
        out_specs=(prompt, reply, prompt, prompt, prompt, reply, reply, reply),
        check_vma=False,
    )
```

```python
import jax
import jax.numpy as jnp
from jax import lax
from jax.experimental import pallas as pl
from jax.experimental.pallas import tpu as pltpu
from jax.sharding import PartitionSpec as P

MESH = pl.DeviceIdType.MESH
F32 = jnp.float32
BF16 = jnp.bfloat16
NY, NX, NZ, NC = 8, 4, 8, 2
E = 128
ROWS = 1024
PROMPT_HEADS = 4
REPLY_HEADS = 2
BLK = 256
SL = E // NY
FAR = [4, 3, 5, 2, 6, 1, 7, 0]
NEAR = [0, 1, 7, 2, 6, 3, 5, 4]

NN = (((1,), (0,)), ((), ()))
NT = (((1,), (1,)), ((), ()))
TN = (((0,), (0,)), ((), ()))


def dot(a, b, dims):
    return lax.dot_general(a, b, dims, preferred_element_type=F32)


def scale_rows(x, first, heads):
    s = lax.broadcasted_iota(jnp.int32, x.shape, 0)
    pos = (first + s // heads).astype(F32)
    return (x.astype(F32) * lax.rsqrt(float(E) * (pos + 1.0))).astype(BF16)


def by_head(x, heads):
    period = lax.broadcasted_iota(jnp.int32, (16, E), 0) & (heads - 1)
    tiles = x.reshape(ROWS // 16, 16, E)
    parts = []
    for h in range(heads):
        keep = jnp.where(period == h, 1.0, 0.0).astype(BF16)
        parts.append((tiles * keep[None]).reshape(ROWS, E))
    return jnp.concatenate(parts, axis=1)


def reply_weighted(c, weight, length):
    s = lax.broadcasted_iota(jnp.int32, c.shape, 0)
    live = (s // REPLY_HEADS) < length
    return (weight * jnp.where(live, c.astype(F32), 0.0)).astype(BF16)


def wait_bytes(view, sem):
    pltpu.make_async_copy(view, view, sem).wait()


def pair_masks(heads):
    a = lax.broadcasted_iota(jnp.int32, (BLK, BLK), 0)
    b = lax.broadcasted_iota(jnp.int32, (BLK, BLK), 1)
    same = ((a ^ b) & (heads - 1)) == 0
    off = jnp.where(same, 1.0, 0.0)
    diag = jnp.where(a >= b, off, 0.0)
    return off.astype(BF16), diag.astype(BF16)


def mixings(left, right, heads, dest):
    off, diag = pair_masks(heads)
    for i in range(ROWS // BLK):
        rows = pl.ds(i * BLK, BLK)
        for j in range(i + 1):
            cols = pl.ds(j * BLK, BLK)
            part = dot(left[i * BLK:(i + 1) * BLK], right[j * BLK:(j + 1) * BLK], NT)
            dest[rows, cols] = part.astype(BF16) * (diag if i == j else off)


def stack_wide(state, heads):
    return jnp.concatenate([state[h * E:(h + 1) * E] for h in range(heads)], axis=1)


def exchange_kernel(
    pq_in, pk_in, pv_in, pc_in, rq_in, rk_in, rv_in, rc_in, weight, length,
    po_out, ro_out, pdq_out, rdq_out, rdk_out, rdv_out, pdk_out, pdv_out, aft_out,
    pq, pk, pv, pc, rq, rk, rv, rc,
    po, ro, pdq, rdq, rdk, rdv, pdk, pdv, aft, bef,
    pqs, pcs, rqs, rcs, rw, mix, gmix, part,
    raw, loc, xr, yt, yr, ys, yb, xs, st, zf, fin, wl, wp, ws, wy, wq, wt, wf,
    in_sem, out_sem,
    x_send, x_recv, y_send, y_recv, b_send, b_recv, s_send, s_recv,
    z_send, z_recv, f_send, f_recv, w_send, w_recv, v_send, v_recv, u_send, u_recv, c_send, c_recv,
):
    y = lax.axis_index("ctx")
    x = lax.axis_index("head")
    r = lax.axis_index("resp")
    z = r // 2
    c = r % 2
    fx = 2 * c + x // 2
    same_column = fx == x
    owner = (y, 2 * (x % 2) + c, 2 * z + x // 2)
    summer = (y, fx, 2 * z + x % 2)

    barrier = pltpu.get_barrier_semaphore()

    loads = [
        pltpu.make_async_copy(src, dst, in_sem.at[n])
        for n, (src, dst) in enumerate((
            (pk_in, pk), (pv_in, pv), (rq_in, rq), (rc_in, rc),
            (pq_in, pq), (pc_in, pc), (rk_in, rk), (rv_in, rv)))
    ]
    for load in loads:
        load.start()

    saves = []

    def save(src, dst):
        copy = pltpu.make_async_copy(src, dst, out_sem.at[len(saves)])
        copy.start()
        saves.append(copy)

    def send(src, dst, send_sem, recv_sem, device):
        pltpu.make_async_remote_copy(
            src_ref=src, dst_ref=dst, send_sem=send_sem, recv_sem=recv_sem,
            device_id=device, device_id_type=MESH).start()

    def signal(device):
        pl.semaphore_signal(barrier, inc=1, device_id=device, device_id_type=MESH)

    @pl.loop(1, NX)
    def _(d):
        signal((y, (x + d) % NX, r))

    @pl.loop(1, NY)
    def _(d):
        signal(((y + d) % NY, x, r))

    @pl.loop(1, NZ * NC)
    def _(d):
        signal((y, x, (r + d) % (NZ * NC)))

    @pl.when(jnp.logical_not(same_column))
    def _():
        signal(owner)
        signal(summer)

    block = y * NX + x
    prompt_first = block * (ROWS // PROMPT_HEADS)
    reply_first = NY * NX * (ROWS // PROMPT_HEADS)

    def states(k, left, right):
        wide = dot(left, by_head(right, PROMPT_HEADS), TN)
        for h in range(PROMPT_HEADS):
            raw[h] = wide[:, h * E:(h + 1) * E].reshape(NY, SL, E)
        for p in range(NY):
            row = (y + FAR[p]) % NY
            for h in range(PROMPT_HEADS):
                loc[k, h, p] = raw[h, row]

    def x_start(k):
        for piece in range(NY // 2):
            span = pl.ds(2 * piece, 2)

            @pl.loop(1, NX)
            def _(d):
                to = (x + d) % NX
                send(loc.at[k, to, span], xr.at[k, x, span],
                     x_send.at[k], x_recv.at[k, piece], (y, to, r))
        xr[k, x] = loc[k, x]

    def y_piece(k, piece):
        wait_bytes(xr.at[k, 0, pl.ds(0, 2 * (NX - 1))], x_recv.at[k, piece])
        for p in (2 * piece, 2 * piece + 1):
            yt[k, p] = (xr[k, 0, p] + xr[k, 1, p]) + (xr[k, 2, p] + xr[k, 3, p])
            if FAR[p]:
                send(yt.at[k, p], yr.at[k, y], y_send.at[k], y_recv.at[k],
                     ((y + FAR[p]) % NY, x, r))
            else:
                yr[k, y] = yt[k, p]

    def b_start(k):
        for rel in FAR[:-1]:
            to = (y + rel) % NY
            back = (NY - rel) % NY
            send(ys.at[k, to], yb.at[k, NEAR.index(back)],
                 b_send.at[k], b_recv.at[k, min(back, NY - back) - 1], (to, x, r))
        yb[k, 0] = ys[k, y]

    def s_piece(k, piece):
        first, count = ((0, 3), (3, 2), (5, 2), (7, 1))[piece]
        wait_bytes(yb.at[k, pl.ds(0, 1 if piece == 3 else 2)], b_recv.at[k, piece])
        for q in range(first, first + count):
            p = FAR.index(NEAR[q])
            running = yb[k, q]
            order = range(NX) if k == 0 else range(NX - 1, -1, -1)
            for n in order:
                xs[k, n, q] = running
                running = running + xr[k, n, p]
        span = pl.ds(first, count)

        @pl.loop(1, NX)
        def _(d):
            to = (x + d) % NX
            send(xs.at[k, to, span], st.at[k, x, span],
                 s_send.at[k], s_recv.at[k], (y, to, r))
        for q in range(first, first + count):
            st[k, x, q] = xs[k, x, q]

    def collect(k, dest):
        wait_bytes(st.at[k, pl.ds(0, NX - 1)], s_recv.at[k])
        for q in range(NY):
            row = (y + NEAR[q]) % NY
            for h in range(PROMPT_HEADS):
                dest[h, row] = st[k, h, q].astype(BF16)

    loads[0].wait()
    loads[1].wait()
    states(0, pk[...], pv[...])

    loads[2].wait()
    loads[3].wait()
    rw[...] = reply_weighted(rc[...], weight[0], length[0])
    rqs[...] = scale_rows(rq[...], reply_first, REPLY_HEADS)
    wide = dot(rqs[...], by_head(rw[...], REPLY_HEADS), TN)
    for i in range(REPLY_HEADS):
        wl[i] = wide[:, i * E:(i + 1) * E].reshape(NY, SL, E)

    near = NX - 1 + NY - 1 + NZ * NC - 1

    @pl.when(same_column)
    def _():
        pl.semaphore_wait(barrier, near)

    @pl.when(jnp.logical_not(same_column))
    def _():
        pl.semaphore_wait(barrier, near + 2)

    send(wl.at[1 - c], wp, c_send, c_recv, (y, x, 2 * z + 1 - c))
    x_start(0)

    loads[4].wait()
    loads[5].wait()
    pqs[...] = scale_rows(pq[...], prompt_first, PROMPT_HEADS)
    states(1, pqs[...], pc[...])
    x_start(1)

    wait_bytes(wp, c_recv)
    ws[...] = wl[c] + wp[...]
    for rel in FAR[:-1]:
        to = (y + rel) % NY
        send(ws.at[to], wy.at[y], w_send, w_recv, (to, x, r))
    wy[y] = ws[y]

    blocks = [(slice(i * BLK, (i + 1) * BLK), slice(0, (i + 1) * BLK), slice(i * BLK, ROWS))
              for i in range(ROWS // BLK)]

    mixings(pqs, pk, PROMPT_HEADS, mix)
    pcs[...] = scale_rows(pc[...], prompt_first, PROMPT_HEADS)
    mixings(pcs, pv, PROMPT_HEADS, gmix)

    for piece in range(3):
        y_piece(0, piece)

    wait_bytes(wy.at[pl.ds(0, NY - 1)], w_recv)
    for rel in FAR[:-1]:
        to = (z + rel) % NZ
        send(wy.at[to], wq.at[z], v_send, v_recv, (y, x, 2 * to + c))
    wq[z] = wy[z]

    y_piece(0, 3)
    for piece in range(NY // 2):
        y_piece(1, piece)

    wait_bytes(yr.at[0, pl.ds(0, NY - 1)], y_recv.at[0])
    running = jnp.zeros((SL, E), F32)
    for n in range(NY):
        ys[0, n] = running
        running = running + yr[0, n]
    zf[z] = running
    b_start(0)

    @pl.loop(1, NZ)
    def _(d):
        send(zf.at[z], zf.at[z], z_send, z_recv, (y, x, 2 * ((z + d) % NZ) + c))

    for rows, upto, onward in blocks:
        part[0, rows] = dot(mix[rows, upto], pv[upto], NN)
        part[1, rows] = dot(gmix[rows, upto], pk[upto], NN)

    wait_bytes(wq.at[pl.ds(0, NZ - 1)], v_recv)
    total = wq[0]
    for n in range(1, NZ):
        total = total + wq[n]
    wt[...] = total

    @pl.when(jnp.logical_not(same_column))
    def _():
        send(wt, wf, u_send, u_recv, owner)

    @pl.when(same_column)
    def _():
        wf[...] = wt[...]

    for rows, upto, onward in blocks:
        pdk[rows] = dot(gmix[onward, rows], pq[onward], TN)
        pdv[rows] = dot(mix[onward, rows], pc[onward], TN)
    save(pdk, pdk_out)
    save(pdv, pdv_out)

    wait_bytes(yr.at[1, pl.ds(0, NY - 1)], y_recv.at[1])

    @pl.when(jnp.logical_not(same_column))
    def _():
        wait_bytes(wf, u_recv)

    running = wf[...]
    for n in reversed(range(NY)):
        ys[1, n] = running
        running = running + yr[1, n]
    b_start(1)

    wait_bytes(zf.at[pl.ds(0, NZ - 1)], z_recv)
    for rel in FAR:
        row = (y + rel) % NY
        for core in range(NC):
            def go():
                send(zf.at[row], fin.at[(x % 2) * NY + y], f_send, f_recv,
                     (row, fx, 2 * z + core))
            if rel:
                go()
            else:
                pl.when(jnp.logical_not(same_column & (c == core)))(go)

    @pl.when(same_column)
    def _():
        fin[(x % 2) * NY + y] = zf[y]

    s_piece(0, 0)
    s_piece(0, 1)
    s_piece(0, 2)
    s_piece(0, 3)

    loads[6].wait()
    loads[7].wait()
    mixings(rqs, rk, REPLY_HEADS, mix)
    rcs[...] = scale_rows(rw[...], reply_first, REPLY_HEADS)
    mixings(rcs, rv, REPLY_HEADS, gmix)

    s_piece(1, 0)
    s_piece(1, 1)
    s_piece(1, 2)
    s_piece(1, 3)

    for rows, upto, onward in blocks:
        rdv[rows] = dot(mix[onward, rows], rw[onward], TN).astype(BF16)
    save(rdv, rdv_out)
    for rows, upto, onward in blocks:
        rdk[rows] = dot(gmix[onward, rows], rq[onward], TN).astype(BF16)
    save(rdk, rdk_out)
    for rows, upto, onward in blocks:
        part[2, rows] = dot(mix[rows, upto], rv[upto], NN)
        part[3, rows] = dot(gmix[rows, upto], rk[upto], NN)

    collect(0, bef)
    before = bef[...].reshape(PROMPT_HEADS * E, E)
    po[...] = (part[0] + dot(by_head(pqs[...], PROMPT_HEADS), before, NN)).astype(BF16)
    save(po, po_out)
    wide = stack_wide(before, PROMPT_HEADS)
    pdq[...] = (part[1] + dot(by_head(pcs[...], PROMPT_HEADS), wide, NT)).astype(BF16)
    save(pdq, pdq_out)

    @pl.when(same_column)
    def _():
        wait_bytes(fin.at[pl.ds(0, 15)], f_recv)

    @pl.when(jnp.logical_not(same_column))
    def _():
        wait_bytes(fin, f_recv)

    final = fin[...].reshape(REPLY_HEADS * E, E).astype(BF16)
    out = part[2] + dot(by_head(rqs[...], REPLY_HEADS), final, NN)
    s = lax.broadcasted_iota(jnp.int32, (ROWS, E), 0)
    ro[...] = jnp.where((s // REPLY_HEADS) < length[0], out, 0.0).astype(BF16)
    save(ro, ro_out)
    wide = stack_wide(final, REPLY_HEADS)
    rdq[...] = (part[3] + dot(by_head(rcs[...], REPLY_HEADS), wide, NT)).astype(BF16)
    save(rdq, rdq_out)

    collect(1, aft)
    save(aft, aft_out)

    for k in range(2):
        wait_bytes(loc.at[k, pl.ds(0, NX - 1)], x_send.at[k])
        wait_bytes(yt.at[k, pl.ds(0, NY - 1)], y_send.at[k])
        wait_bytes(ys.at[k, pl.ds(0, NY - 1)], b_send.at[k])
        wait_bytes(xs.at[k, pl.ds(0, NX - 1)], s_send.at[k])
    wait_bytes(wp, c_send)
    wait_bytes(wy.at[pl.ds(0, NY - 1)], w_send)
    wait_bytes(wq.at[pl.ds(0, NZ - 1)], v_send)
    wait_bytes(zf.at[pl.ds(0, NZ - 1)], z_send)

    @pl.when(same_column)
    def _():
        wait_bytes(fin.at[pl.ds(0, 15)], f_send)

    @pl.when(jnp.logical_not(same_column))
    def _():
        wait_bytes(fin, f_send)
        wait_bytes(wt, u_send)

    for copy in saves:
        copy.wait()


def exchange(*args):
    whole = pl.BlockSpec(memory_space=pl.ANY)
    smem = pl.BlockSpec(memory_space=pltpu.SMEM)
    dma = pltpu.SemaphoreType.DMA
    heads = pltpu.VMEM((2, NX, NY, SL, E), F32)
    narrow = pltpu.VMEM((ROWS, E), BF16)
    wide = pltpu.VMEM((ROWS, E), F32)
    slices = pltpu.VMEM((2, NY, SL, E), F32)
    return pl.pallas_call(
        exchange_kernel,
        out_shape=tuple(
            [jax.ShapeDtypeStruct((ROWS, E), BF16)] * 6
            + [jax.ShapeDtypeStruct((ROWS, E), F32)] * 2
            + [jax.ShapeDtypeStruct((PROMPT_HEADS, NY, SL, E), BF16)]),
        in_specs=[whole] * 8 + [smem] * 2,
        out_specs=tuple([whole] * 9),
        scratch_shapes=[narrow] * 14 + [wide] * 2 + [
            pltpu.VMEM((PROMPT_HEADS, NY, SL, E), BF16),
            pltpu.VMEM((PROMPT_HEADS, NY, SL, E), BF16),
        ] + [narrow] * 5 + [
            pltpu.VMEM((ROWS, ROWS), BF16),
            pltpu.VMEM((ROWS, ROWS), BF16),
            pltpu.VMEM((4, ROWS, E), F32),
            pltpu.VMEM((NX, NY, SL, E), F32),
            heads, heads,
            slices, slices, slices, slices,
            heads, heads,
            pltpu.VMEM((NZ, SL, E), F32),
            pltpu.VMEM((16, SL, E), F32),
            slices,
            pltpu.VMEM((NY, SL, E), F32),
            pltpu.VMEM((NY, SL, E), F32),
            pltpu.VMEM((NY, SL, E), F32),
            pltpu.VMEM((NZ, SL, E), F32),
            pltpu.VMEM((SL, E), F32),
            pltpu.VMEM((SL, E), F32),
            dma((8,)), dma((9,)),
            dma((2,)), dma((2, 4)), dma((2,)), dma((2,)),
            dma((2,)), dma((2, 4)), dma((2,)), dma((2,)),
            dma, dma, dma, dma, dma, dma, dma, dma, dma, dma, dma, dma,
        ],
        compiler_params=pltpu.CompilerParams(
            collective_id=0, has_side_effects=True),
        name="exchange",
    )(*args)


def finish_kernel(
    po_in, ro_in, pdq_in, rdq_in, rdk_in, rdv_in, pdk_in, pdv_in, aft_in, pk_in, pv_in,
    po_out, ro_out, pdq_out, rdq_out, rdk_out, rdv_out, pdk_out, pdv_out,
    po, ro, pdq, rdq, rdk, rdv, kpart, vpart, aft, pk, pv, pdk, pdv, in_sem, out_sem,
):
    ins = (aft_in, pv_in, pdk_in, pk_in, pdv_in, po_in, ro_in, pdq_in, rdq_in, rdk_in, rdv_in)
    held = (aft, pv, kpart, pk, vpart, po, ro, pdq, rdq, rdk, rdv)
    outs = (po_out, ro_out, pdq_out, rdq_out, rdk_out, rdv_out)
    loads = [pltpu.make_async_copy(src, dst, in_sem.at[n])
             for n, (src, dst) in enumerate(zip(ins, held))]
    for load in loads:
        load.start()
    saves = []

    def save(src, dst):
        copy = pltpu.make_async_copy(src, dst, out_sem.at[len(saves)])
        copy.start()
        saves.append(copy)

    loads[0].wait()
    loads[1].wait()
    wide = stack_wide(aft[...], PROMPT_HEADS)
    grad = dot(by_head(pv[...], PROMPT_HEADS), wide, NT)
    loads[2].wait()
    pdk[...] = (kpart[...] + grad).astype(BF16)
    save(pdk, pdk_out)
    loads[3].wait()
    grad = dot(by_head(pk[...], PROMPT_HEADS), aft[...], NN)
    loads[4].wait()
    pdv[...] = (vpart[...] + grad).astype(BF16)
    save(pdv, pdv_out)
    for n in range(6):
        loads[5 + n].wait()
        save(held[5 + n], outs[n])
    for copy in saves:
        copy.wait()


def finish(*args):
    whole = pl.BlockSpec(memory_space=pl.ANY)
    narrow = pltpu.VMEM((ROWS, E), BF16)
    wide = pltpu.VMEM((ROWS, E), F32)
    return pl.pallas_call(
        finish_kernel,
        out_shape=tuple([jax.ShapeDtypeStruct((ROWS, E), BF16)] * 8),
        in_specs=[whole] * 11,
        out_specs=tuple([whole] * 8),
        scratch_shapes=[narrow] * 6 + [wide] * 2 + [
            pltpu.VMEM((PROMPT_HEADS * E, E), BF16)] + [narrow] * 4 + [
            pltpu.SemaphoreType.DMA((11,)), pltpu.SemaphoreType.DMA((8,))],
        name="finish",
    )(*args)


def shards(
    prompt_query, prompt_key, prompt_value, prompt_cotangent,
    reply_query, reply_key, reply_value, reply_cotangent,
    reply_weight, reply_length,
):
    prompt_shape = prompt_query.shape
    reply_shape = reply_query.shape
    pq, pk, pv, pc, rq, rk, rv, rc = [
        a.reshape(ROWS, E)
        for a in (prompt_query, prompt_key, prompt_value, prompt_cotangent,
                  reply_query, reply_key, reply_value, reply_cotangent)
    ]
    parts = exchange(pq, pk, pv, pc, rq, rk, rv, rc, reply_weight, reply_length)
    after = parts[-1].reshape(PROMPT_HEADS * E, E)
    po, ro, pdq, rdq, rdk, rdv, pdk, pdv = finish(*parts[:-1], after, pk, pv)
    return (
        po.reshape(prompt_shape), ro.reshape(reply_shape),
        pdq.reshape(prompt_shape), pdk.reshape(prompt_shape), pdv.reshape(prompt_shape),
        rdq.reshape(reply_shape), rdk.reshape(reply_shape), rdv.reshape(reply_shape),
    )


def solution(mesh):
    prompt = P(("ctx", "head"), "resp", None)
    reply = P("resp", None, ("ctx", "head"), None)
    placed = (prompt,) * 4 + (reply,) * 4 + (P("resp"), P("resp"))
    return jax.shard_map(
        shards,
        mesh=mesh,
        in_specs=placed,
        out_specs=(prompt, reply, prompt, prompt, prompt, reply, reply, reply),
        check_vma=False,
    )
```

```python
import jax
import jax.numpy as jnp
from jax import lax
from jax.experimental import pallas as pl
from jax.experimental.pallas import tpu as pltpu
from jax.sharding import PartitionSpec as P

MESH = pl.DeviceIdType.MESH
F32 = jnp.float32
BF16 = jnp.bfloat16
NY, NX, NZ, NC = 8, 4, 8, 2
E = 128
ROWS = 1024
PROMPT_HEADS = 4
REPLY_HEADS = 2
BLK = 256
SL = E // NY
FAR = [4, 3, 5, 2, 6, 1, 7, 0]
NEAR = [0, 1, 7, 2, 6, 3, 5, 4]

NN = (((1,), (0,)), ((), ()))
NT = (((1,), (1,)), ((), ()))
TN = (((0,), (0,)), ((), ()))


def dot(a, b, dims):
    return lax.dot_general(a, b, dims, preferred_element_type=F32)


def scale_rows(x, first, heads):
    s = lax.broadcasted_iota(jnp.int32, x.shape, 0)
    pos = (first + s // heads).astype(F32)
    return (x.astype(F32) * lax.rsqrt(float(E) * (pos + 1.0))).astype(BF16)


def by_head(x, heads):
    period = lax.broadcasted_iota(jnp.int32, (16, E), 0) & (heads - 1)
    tiles = x.reshape(ROWS // 16, 16, E)
    parts = []
    for h in range(heads):
        keep = jnp.where(period == h, 1.0, 0.0).astype(BF16)
        parts.append((tiles * keep[None]).reshape(ROWS, E))
    return jnp.concatenate(parts, axis=1)


def reply_weighted(c, weight, length):
    s = lax.broadcasted_iota(jnp.int32, c.shape, 0)
    live = (s // REPLY_HEADS) < length
    return (weight * jnp.where(live, c.astype(F32), 0.0)).astype(BF16)


def wait_bytes(view, sem):
    pltpu.make_async_copy(view, view, sem).wait()


def pair_masks(heads):
    a = lax.broadcasted_iota(jnp.int32, (BLK, BLK), 0)
    b = lax.broadcasted_iota(jnp.int32, (BLK, BLK), 1)
    same = ((a ^ b) & (heads - 1)) == 0
    off = jnp.where(same, 1.0, 0.0)
    diag = jnp.where(a >= b, off, 0.0)
    return off.astype(BF16), diag.astype(BF16)


def mixings(left, right, heads, dest):
    off, diag = pair_masks(heads)
    for i in range(ROWS // BLK):
        rows = pl.ds(i * BLK, BLK)
        for j in range(i + 1):
            cols = pl.ds(j * BLK, BLK)
            part = dot(left[i * BLK:(i + 1) * BLK], right[j * BLK:(j + 1) * BLK], NT)
            dest[rows, cols] = part.astype(BF16) * (diag if i == j else off)


def stack_wide(state, heads):
    return jnp.concatenate([state[h * E:(h + 1) * E] for h in range(heads)], axis=1)


def exchange_kernel(
    pq_in, pk_in, pv_in, pc_in, rq_in, rk_in, rv_in, rc_in, weight, length,
    po_out, ro_out, pdq_out, rdq_out, rdk_out, rdv_out, pdk_out, pdv_out, aft_out,
    pq, pk, pv, pc, rq, rk, rv, rc,
    po, ro, pdq, rdq, rdk, rdv, pdk, pdv, aft, bef,
    pqs, pcs, rqs, rcs, rw, mix, gmix, part,
    raw, loc, xr, yt, yr, ys, yb, xs, st, zf, fin, wl, wp, ws, wy, wq, wt, wf,
    in_sem, out_sem,
    x_send, x_recv, y_send, y_recv, b_send, b_recv, s_send, s_recv,
    z_send, z_recv, f_send, f_recv, w_send, w_recv, v_send, v_recv, u_send, u_recv, c_send, c_recv,
):
    y = lax.axis_index("ctx")
    x = lax.axis_index("head")
    r = lax.axis_index("resp")
    z = r // 2
    c = r % 2
    fx = 2 * c + x // 2
    same_column = fx == x
    owner = (y, 2 * (x % 2) + c, 2 * z + x // 2)
    summer = (y, fx, 2 * z + x % 2)

    barrier = pltpu.get_barrier_semaphore()

    loads = [
        pltpu.make_async_copy(src, dst, in_sem.at[n])
        for n, (src, dst) in enumerate((
            (pk_in, pk), (pv_in, pv), (rq_in, rq), (rc_in, rc),
            (pq_in, pq), (pc_in, pc), (rk_in, rk), (rv_in, rv)))
    ]
    for load in loads:
        load.start()

    saves = []

    def save(src, dst):
        copy = pltpu.make_async_copy(src, dst, out_sem.at[len(saves)])
        copy.start()
        saves.append(copy)

    def send(src, dst, send_sem, recv_sem, device):
        pltpu.make_async_remote_copy(
            src_ref=src, dst_ref=dst, send_sem=send_sem, recv_sem=recv_sem,
            device_id=device, device_id_type=MESH).start()

    def signal(device):
        pl.semaphore_signal(barrier, inc=1, device_id=device, device_id_type=MESH)

    @pl.loop(1, NX)
    def _(d):
        signal((y, (x + d) % NX, r))

    @pl.loop(1, NY)
    def _(d):
        signal(((y + d) % NY, x, r))

    @pl.loop(1, NZ * NC)
    def _(d):
        signal((y, x, (r + d) % (NZ * NC)))

    @pl.when(jnp.logical_not(same_column))
    def _():
        signal(owner)
        signal(summer)

    block = y * NX + x
    prompt_first = block * (ROWS // PROMPT_HEADS)
    reply_first = NY * NX * (ROWS // PROMPT_HEADS)

    def states(k, left, right):
        wide = dot(left, by_head(right, PROMPT_HEADS), TN)
        for h in range(PROMPT_HEADS):
            raw[h] = wide[:, h * E:(h + 1) * E].reshape(NY, SL, E)
        for p in range(NY):
            row = (y + FAR[p]) % NY
            for h in range(PROMPT_HEADS):
                loc[k, h, p] = raw[h, row]

    def x_start(k):
        for piece in range(NY // 2):
            span = pl.ds(2 * piece, 2)

            @pl.loop(1, NX)
            def _(d):
                to = (x + d) % NX
                send(loc.at[k, to, span], xr.at[k, x, span],
                     x_send.at[k], x_recv.at[k, piece], (y, to, r))
        xr[k, x] = loc[k, x]

    def y_piece(k, piece):
        wait_bytes(xr.at[k, 0, pl.ds(0, 2 * (NX - 1))], x_recv.at[k, piece])
        for p in (2 * piece, 2 * piece + 1):
            yt[k, p] = (xr[k, 0, p] + xr[k, 1, p]) + (xr[k, 2, p] + xr[k, 3, p])
            if FAR[p]:
                send(yt.at[k, p], yr.at[k, y], y_send.at[k], y_recv.at[k],
                     ((y + FAR[p]) % NY, x, r))
            else:
                yr[k, y] = yt[k, p]

    def b_start(k):
        for rel in FAR[:-1]:
            to = (y + rel) % NY
            back = (NY - rel) % NY
            send(ys.at[k, to], yb.at[k, NEAR.index(back)],
                 b_send.at[k], b_recv.at[k, min(back, NY - back) - 1], (to, x, r))
        yb[k, 0] = ys[k, y]

    def s_piece(k, piece):
        first, count = ((0, 3), (3, 2), (5, 2), (7, 1))[piece]
        wait_bytes(yb.at[k, pl.ds(0, 1 if piece == 3 else 2)], b_recv.at[k, piece])
        for q in range(first, first + count):
            p = FAR.index(NEAR[q])
            running = yb[k, q]
            order = range(NX) if k == 0 else range(NX - 1, -1, -1)
            for n in order:
                xs[k, n, q] = running
                running = running + xr[k, n, p]
        span = pl.ds(first, count)

        @pl.loop(1, NX)
        def _(d):
            to = (x + d) % NX
            send(xs.at[k, to, span], st.at[k, x, span],
                 s_send.at[k], s_recv.at[k], (y, to, r))
        for q in range(first, first + count):
            st[k, x, q] = xs[k, x, q]

    def collect(k, dest):
        wait_bytes(st.at[k, pl.ds(0, NX - 1)], s_recv.at[k])
        for q in range(NY):
            row = (y + NEAR[q]) % NY
            for h in range(PROMPT_HEADS):
                dest[h, row] = st[k, h, q].astype(BF16)

    loads[0].wait()
    loads[1].wait()
    states(0, pk[...], pv[...])

    loads[2].wait()
    loads[3].wait()
    rw[...] = reply_weighted(rc[...], weight[0], length[0])
    rqs[...] = scale_rows(rq[...], reply_first, REPLY_HEADS)
    wide = dot(rqs[...], by_head(rw[...], REPLY_HEADS), TN)
    for i in range(REPLY_HEADS):
        wl[i] = wide[:, i * E:(i + 1) * E].reshape(NY, SL, E)

    near = NX - 1 + NY - 1 + NZ * NC - 1

    @pl.when(same_column)
    def _():
        pl.semaphore_wait(barrier, near)

    @pl.when(jnp.logical_not(same_column))
    def _():
        pl.semaphore_wait(barrier, near + 2)

    send(wl.at[1 - c], wp, c_send, c_recv, (y, x, 2 * z + 1 - c))
    x_start(0)

    loads[4].wait()
    loads[5].wait()
    pqs[...] = scale_rows(pq[...], prompt_first, PROMPT_HEADS)
    states(1, pqs[...], pc[...])
    x_start(1)

    wait_bytes(wp, c_recv)
    ws[...] = wl[c] + wp[...]
    for rel in FAR[:-1]:
        to = (y + rel) % NY
        send(ws.at[to], wy.at[y], w_send, w_recv, (to, x, r))
    wy[y] = ws[y]

    blocks = [(slice(i * BLK, (i + 1) * BLK), slice(0, (i + 1) * BLK), slice(i * BLK, ROWS))
              for i in range(ROWS // BLK)]

    mixings(pqs, pk, PROMPT_HEADS, mix)
    pcs[...] = scale_rows(pc[...], prompt_first, PROMPT_HEADS)
    mixings(pcs, pv, PROMPT_HEADS, gmix)

    for piece in range(3):
        y_piece(0, piece)

    wait_bytes(wy.at[pl.ds(0, NY - 1)], w_recv)
    for rel in FAR[:-1]:
        to = (z + rel) % NZ
        send(wy.at[to], wq.at[z], v_send, v_recv, (y, x, 2 * to + c))
    wq[z] = wy[z]

    y_piece(0, 3)
    for piece in range(NY // 2):
        y_piece(1, piece)

    wait_bytes(yr.at[0, pl.ds(0, NY - 1)], y_recv.at[0])
    running = jnp.zeros((SL, E), F32)
    for n in range(NY):
        ys[0, n] = running
        running = running + yr[0, n]
    zf[z] = running
    b_start(0)

    @pl.loop(1, NZ)
    def _(d):
        send(zf.at[z], zf.at[z], z_send, z_recv, (y, x, 2 * ((z + d) % NZ) + c))

    for rows, upto, onward in blocks:
        part[0, rows] = dot(mix[rows, upto], pv[upto], NN)
        part[1, rows] = dot(gmix[rows, upto], pk[upto], NN)

    wait_bytes(wq.at[pl.ds(0, NZ - 1)], v_recv)
    total = wq[0]
    for n in range(1, NZ):
        total = total + wq[n]
    wt[...] = total

    @pl.when(jnp.logical_not(same_column))
    def _():
        send(wt, wf, u_send, u_recv, owner)

    @pl.when(same_column)
    def _():
        wf[...] = wt[...]

    for rows, upto, onward in blocks:
        pdk[rows] = dot(gmix[onward, rows], pq[onward], TN)
        pdv[rows] = dot(mix[onward, rows], pc[onward], TN)
    save(pdk, pdk_out)
    save(pdv, pdv_out)

    @pl.when(c == 1)
    def _():
        for piece in range(4):
            s_piece(0, piece)

    wait_bytes(yr.at[1, pl.ds(0, NY - 1)], y_recv.at[1])

    @pl.when(jnp.logical_not(same_column))
    def _():
        wait_bytes(wf, u_recv)

    running = wf[...]
    for n in reversed(range(NY)):
        ys[1, n] = running
        running = running + yr[1, n]
    b_start(1)

    wait_bytes(zf.at[pl.ds(0, NZ - 1)], z_recv)
    for rel in FAR:
        row = (y + rel) % NY
        for core in range(NC):
            def go():
                send(zf.at[row], fin.at[(x % 2) * NY + y], f_send, f_recv,
                     (row, fx, 2 * z + core))
            if rel:
                go()
            else:
                pl.when(jnp.logical_not(same_column & (c == core)))(go)

    @pl.when(same_column)
    def _():
        fin[(x % 2) * NY + y] = zf[y]

    @pl.when(c == 0)
    def _():
        for piece in range(4):
            s_piece(0, piece)

    loads[6].wait()
    loads[7].wait()
    mixings(rqs, rk, REPLY_HEADS, mix)
    rcs[...] = scale_rows(rw[...], reply_first, REPLY_HEADS)
    mixings(rcs, rv, REPLY_HEADS, gmix)

    s_piece(1, 0)
    s_piece(1, 1)
    s_piece(1, 2)
    s_piece(1, 3)

    for rows, upto, onward in blocks:
        rdv[rows] = dot(mix[onward, rows], rw[onward], TN).astype(BF16)
    save(rdv, rdv_out)
    for rows, upto, onward in blocks:
        rdk[rows] = dot(gmix[onward, rows], rq[onward], TN).astype(BF16)
    save(rdk, rdk_out)
    for rows, upto, onward in blocks:
        part[2, rows] = dot(mix[rows, upto], rv[upto], NN)
        part[3, rows] = dot(gmix[rows, upto], rk[upto], NN)

    collect(0, bef)
    before = bef[...].reshape(PROMPT_HEADS * E, E)
    po[...] = (part[0] + dot(by_head(pqs[...], PROMPT_HEADS), before, NN)).astype(BF16)
    save(po, po_out)
    wide = stack_wide(before, PROMPT_HEADS)
    pdq[...] = (part[1] + dot(by_head(pcs[...], PROMPT_HEADS), wide, NT)).astype(BF16)
    save(pdq, pdq_out)

    @pl.when(same_column)
    def _():
        wait_bytes(fin.at[pl.ds(0, 15)], f_recv)

    @pl.when(jnp.logical_not(same_column))
    def _():
        wait_bytes(fin, f_recv)

    final = fin[...].reshape(REPLY_HEADS * E, E).astype(BF16)
    out = part[2] + dot(by_head(rqs[...], REPLY_HEADS), final, NN)
    s = lax.broadcasted_iota(jnp.int32, (ROWS, E), 0)
    ro[...] = jnp.where((s // REPLY_HEADS) < length[0], out, 0.0).astype(BF16)
    save(ro, ro_out)
    wide = stack_wide(final, REPLY_HEADS)
    rdq[...] = (part[3] + dot(by_head(rcs[...], REPLY_HEADS), wide, NT)).astype(BF16)
    save(rdq, rdq_out)

    collect(1, aft)
    save(aft, aft_out)

    for k in range(2):
        wait_bytes(loc.at[k, pl.ds(0, NX - 1)], x_send.at[k])
        wait_bytes(yt.at[k, pl.ds(0, NY - 1)], y_send.at[k])
        wait_bytes(ys.at[k, pl.ds(0, NY - 1)], b_send.at[k])
        wait_bytes(xs.at[k, pl.ds(0, NX - 1)], s_send.at[k])
    wait_bytes(wp, c_send)
    wait_bytes(wy.at[pl.ds(0, NY - 1)], w_send)
    wait_bytes(wq.at[pl.ds(0, NZ - 1)], v_send)
    wait_bytes(zf.at[pl.ds(0, NZ - 1)], z_send)

    @pl.when(same_column)
    def _():
        wait_bytes(fin.at[pl.ds(0, 15)], f_send)

    @pl.when(jnp.logical_not(same_column))
    def _():
        wait_bytes(fin, f_send)
        wait_bytes(wt, u_send)

    for copy in saves:
        copy.wait()


def exchange(*args):
    whole = pl.BlockSpec(memory_space=pl.ANY)
    smem = pl.BlockSpec(memory_space=pltpu.SMEM)
    dma = pltpu.SemaphoreType.DMA
    heads = pltpu.VMEM((2, NX, NY, SL, E), F32)
    narrow = pltpu.VMEM((ROWS, E), BF16)
    wide = pltpu.VMEM((ROWS, E), F32)
    slices = pltpu.VMEM((2, NY, SL, E), F32)
    return pl.pallas_call(
        exchange_kernel,
        out_shape=tuple(
            [jax.ShapeDtypeStruct((ROWS, E), BF16)] * 6
            + [jax.ShapeDtypeStruct((ROWS, E), F32)] * 2
            + [jax.ShapeDtypeStruct((PROMPT_HEADS, NY, SL, E), BF16)]),
        in_specs=[whole] * 8 + [smem] * 2,
        out_specs=tuple([whole] * 9),
        scratch_shapes=[narrow] * 14 + [wide] * 2 + [
            pltpu.VMEM((PROMPT_HEADS, NY, SL, E), BF16),
            pltpu.VMEM((PROMPT_HEADS, NY, SL, E), BF16),
        ] + [narrow] * 5 + [
            pltpu.VMEM((ROWS, ROWS), BF16),
            pltpu.VMEM((ROWS, ROWS), BF16),
            pltpu.VMEM((4, ROWS, E), F32),
            pltpu.VMEM((NX, NY, SL, E), F32),
            heads, heads,
            slices, slices, slices, slices,
            heads, heads,
            pltpu.VMEM((NZ, SL, E), F32),
            pltpu.VMEM((16, SL, E), F32),
            slices,
            pltpu.VMEM((NY, SL, E), F32),
            pltpu.VMEM((NY, SL, E), F32),
            pltpu.VMEM((NY, SL, E), F32),
            pltpu.VMEM((NZ, SL, E), F32),
            pltpu.VMEM((SL, E), F32),
            pltpu.VMEM((SL, E), F32),
            dma((8,)), dma((9,)),
            dma((2,)), dma((2, 4)), dma((2,)), dma((2,)),
            dma((2,)), dma((2, 4)), dma((2,)), dma((2,)),
            dma, dma, dma, dma, dma, dma, dma, dma, dma, dma, dma, dma,
        ],
        compiler_params=pltpu.CompilerParams(
            collective_id=0, has_side_effects=True),
        name="exchange",
    )(*args)


def finish_kernel(
    po_in, ro_in, pdq_in, rdq_in, rdk_in, rdv_in, pdk_in, pdv_in, aft_in, pk_in, pv_in,
    po_out, ro_out, pdq_out, rdq_out, rdk_out, rdv_out, pdk_out, pdv_out,
    po, ro, pdq, rdq, rdk, rdv, kpart, vpart, aft, pk, pv, pdk, pdv, in_sem, out_sem,
):
    ins = (aft_in, pv_in, pdk_in, pk_in, pdv_in, po_in, ro_in, pdq_in, rdq_in, rdk_in, rdv_in)
    held = (aft, pv, kpart, pk, vpart, po, ro, pdq, rdq, rdk, rdv)
    outs = (po_out, ro_out, pdq_out, rdq_out, rdk_out, rdv_out)
    loads = [pltpu.make_async_copy(src, dst, in_sem.at[n])
             for n, (src, dst) in enumerate(zip(ins, held))]
    for load in loads:
        load.start()
    saves = []

    def save(src, dst):
        copy = pltpu.make_async_copy(src, dst, out_sem.at[len(saves)])
        copy.start()
        saves.append(copy)

    loads[0].wait()
    loads[1].wait()
    wide = stack_wide(aft[...], PROMPT_HEADS)
    grad = dot(by_head(pv[...], PROMPT_HEADS), wide, NT)
    loads[2].wait()
    pdk[...] = (kpart[...] + grad).astype(BF16)
    save(pdk, pdk_out)
    loads[3].wait()
    grad = dot(by_head(pk[...], PROMPT_HEADS), aft[...], NN)
    loads[4].wait()
    pdv[...] = (vpart[...] + grad).astype(BF16)
    save(pdv, pdv_out)
    for n in range(6):
        loads[5 + n].wait()
        save(held[5 + n], outs[n])
    for copy in saves:
        copy.wait()


def finish(*args):
    whole = pl.BlockSpec(memory_space=pl.ANY)
    narrow = pltpu.VMEM((ROWS, E), BF16)
    wide = pltpu.VMEM((ROWS, E), F32)
    return pl.pallas_call(
        finish_kernel,
        out_shape=tuple([jax.ShapeDtypeStruct((ROWS, E), BF16)] * 8),
        in_specs=[whole] * 11,
        out_specs=tuple([whole] * 8),
        scratch_shapes=[narrow] * 6 + [wide] * 2 + [
            pltpu.VMEM((PROMPT_HEADS * E, E), BF16)] + [narrow] * 4 + [
            pltpu.SemaphoreType.DMA((11,)), pltpu.SemaphoreType.DMA((8,))],
        name="finish",
    )(*args)


def shards(
    prompt_query, prompt_key, prompt_value, prompt_cotangent,
    reply_query, reply_key, reply_value, reply_cotangent,
    reply_weight, reply_length,
):
    prompt_shape = prompt_query.shape
    reply_shape = reply_query.shape
    pq, pk, pv, pc, rq, rk, rv, rc = [
        a.reshape(ROWS, E)
        for a in (prompt_query, prompt_key, prompt_value, prompt_cotangent,
                  reply_query, reply_key, reply_value, reply_cotangent)
    ]
    parts = exchange(pq, pk, pv, pc, rq, rk, rv, rc, reply_weight, reply_length)
    after = parts[-1].reshape(PROMPT_HEADS * E, E)
    po, ro, pdq, rdq, rdk, rdv, pdk, pdv = finish(*parts[:-1], after, pk, pv)
    return (
        po.reshape(prompt_shape), ro.reshape(reply_shape),
        pdq.reshape(prompt_shape), pdk.reshape(prompt_shape), pdv.reshape(prompt_shape),
        rdq.reshape(reply_shape), rdk.reshape(reply_shape), rdv.reshape(reply_shape),
    )


def solution(mesh):
    prompt = P(("ctx", "head"), "resp", None)
    reply = P("resp", None, ("ctx", "head"), None)
    placed = (prompt,) * 4 + (reply,) * 4 + (P("resp"), P("resp"))
    return jax.shard_map(
        shards,
        mesh=mesh,
        in_specs=placed,
        out_specs=(prompt, reply, prompt, prompt, prompt, reply, reply, reply),
        check_vma=False,
    )
```
